32 devices in a mesh: grp: 2 (over core), batch: 16 (over z, y, x).
Axes of the slice: x: 2, y: 2, z: 4, core: 2. Of those that a mesh axis runs over, the one named last changes fastest.
Arguments:
- latent: bfloat16 [286720, 256], P(('grp', 'batch')), may hold values from -6 to 6
- future_latent: bfloat16 [286720, 256], P(('grp', 'batch')), may hold values from -6 to 6
- actions: int32 [286720], P(('grp', 'batch')), may hold values from 0 to 3
- codes: int32 [286720], P(('grp', 'batch')), may hold values from 0 to 31
- lengths: int32 [57344], P(('grp', 'batch')), may hold values from 1 to 5
- w_lat: bfloat16 [256, 256], replicated, may hold values from -0.375 to 0.375
- w_act: bfloat16 [4, 256], replicated, may hold values from -4 to 4
- gain_input: float32 [256], replicated, may hold values from 0.1 to 1.9
- gain_block: float32 [256], replicated, may hold values from 0.1 to 1.9
- w_one: bfloat16 [256, 256], replicated, may hold values from -0.375 to 0.375
- w_two: bfloat16 [256, 256], replicated, may hold values from -0.5 to 0.5
- gain_head: float32 [256], replicated, may hold values from 0.1 to 1.9
- w_chance: bfloat16 [256, 32], replicated, may hold values from -0.5 to 0.5
- w_value: bfloat16 [256, 601], replicated, may hold values from -0.5 to 0.5
- w_target: bfloat16 [256, 601], replicated, may hold values from -0.5 to 0.5
Outputs:
- grad_latent: float32 [286720, 256], P(('grp', 'batch'))
- grad_w_lat: float32 [256, 256], replicated
- grad_w_act: float32 [4, 256], replicated
- grad_gain_input: float32 [256], replicated
- grad_gain_block: float32 [256], replicated
- grad_w_one: float32 [256, 256], replicated
- grad_w_two: float32 [256, 256], replicated
- grad_gain_head: float32 [256], replicated
- grad_w_chance: float32 [256, 32], replicated
- grad_w_value: float32 [256, 601], replicated
The draws below stay inside these ranges and needn't reach their ends.
All inputs are finite; a program needn't handle non-finite values.
Results may differ from the reference program's by a relative error of at most 0.007.
The reference program's roundings to bfloat16 on the way count: a program that leaves them out, or rounds other values in their place, can miss the bound.
Values may be sent and summed in bfloat16 or wider, within the bound.
No kernel may reach another device: no remote copies, remote signals or barrier semaphores. Data moves between devices by JAX's collectives and lax.ppermute only.
A program may use at most 256 MiB of HBM per device.

```python
import jax
import jax.numpy as jnp
from jax import lax

D = 256
ACTIONS = 4
CODES = 32
BINS = 601
UNROLL = 5
TRAJ = 57344
ROWS = 286720
N_GRP = 2
N_BATCH = 16


def with_ends(entries, own_key, low, high):
    dims = entries.shape
    index_at = [jax.random.randint(jax.random.fold_in(own_key, axis), (), 0, dims[axis]) for axis in range(len(dims))]
    entries = entries.at[tuple(index_at)].set(low)
    longest = dims.index(max(dims))
    index_at[longest] = (index_at[longest] + 1) % dims[longest]
    return entries.at[tuple(index_at)].set(high)


def steps_of(own_key, shape, cuts, least, high):
    level, own = 1.0, jax.random.fold_in(own_key, 6)
    for position, shards_of in cuts:
        draws = jnp.exp(jax.random.uniform(jax.random.fold_in(own, position), (shards_of,), jnp.float32, least / len(cuts), high / len(cuts)))
        level = level * jnp.repeat(draws, shape[position] // shards_of).reshape([-1 if axis == position else 1 for axis in range(len(shape))])
    return level


def noise(rng, dims, spread, bound, cuts=(), kind=jnp.bfloat16):
    level = steps_of(rng, dims, cuts, -0.22, 0.18) if cuts else 1.0
    result = jax.random.normal(rng, dims, jnp.float32) * spread * level
    return jnp.minimum(jnp.maximum(result, -bound), bound).astype(kind)


def setup_inputs(seed: int = 0) -> dict:
    splits = jax.random.split(jax.random.key(seed), 16)
    return {
        "latent": noise(splits[0], (ROWS, D), 1.0, 6.0, ((0, 32),)),
        "future_latent": noise(splits[1], (ROWS, D), 1.0, 6.0, ((0, 32),)),
        "actions": with_ends(jax.random.randint(splits[2], (ROWS,), 0, ACTIONS), jax.random.fold_in(splits[2], 1), 0, ACTIONS - 1).astype(jnp.int32),
        "codes": with_ends(jax.random.randint(splits[3], (ROWS,), 0, CODES), jax.random.fold_in(splits[3], 1), 0, CODES - 1).astype(jnp.int32),
        "lengths": with_ends(jax.random.randint(splits[4], (TRAJ,), 1, UNROLL + 1), jax.random.fold_in(splits[4], 1), 1, UNROLL).astype(jnp.int32),
        "w_lat": noise(splits[5], (D, D), D ** -0.5, 0.375),
        "w_act": noise(splits[6], (ACTIONS, D), 1.0, 4.0),
        "gain_input": jnp.clip(1.0 + 0.18 * jax.random.normal(splits[7], (D,), jnp.float32), 0.1, 1.9),
        "gain_block": jnp.clip(1.0 + 0.18 * jax.random.normal(splits[8], (D,), jnp.float32), 0.1, 1.9),
        "w_one": noise(splits[9], (D, D), D ** -0.5, 0.375),
        "w_two": noise(splits[10], (D, D), (D // 2) ** -0.5, 0.5),
        "gain_head": jnp.clip(1.0 + 0.18 * jax.random.normal(splits[11], (D,), jnp.float32), 0.1, 1.9),
        "w_chance": noise(splits[12], (D, CODES), (D // 2) ** -0.5, 0.5),
        "w_value": noise(splits[13], (D, BINS), (D // 2) ** -0.5, 0.5),
        "w_target": noise(splits[14], (D, BINS), (D // 2) ** -0.5, 0.5),
    }


@jax.custom_vjp
def low(v):
    return lax.optimization_barrier(v.astype(jnp.bfloat16)).astype(jnp.float32)

@jax.custom_vjp
def low_back(v):
    return v

def low_keep(v):
    return (low(v), None)

def low_pass(kept, grad):
    return (grad,)

def back_keep(v):
    return (v, None)

def back_low(kept, grad):
    return (low(grad),)
low.defvjp(low_keep, low_pass)
low_back.defvjp(back_keep, back_low)
EPSILON = 1e-05

def matmul(left, right):
    return jnp.dot(left, right, precision=lax.Precision.HIGHEST, preferred_element_type=jnp.float32)

def layer_norm(value, gain):
    center = value - lax.optimization_barrier(jnp.mean(value, axis=1, keepdims=True))
    scaled = lax.rsqrt(lax.optimization_barrier(jnp.mean(center * center, axis=1, keepdims=True)) + EPSILON)
    return center * scaled * gain

def block_loss(params, latent, actions, codes, target, weight):
    w_lat, w_act, gain_input, gain_block, w_one, w_two, gain_head, w_chance, w_value = params
    onehot = jax.nn.one_hot(actions, ACTIONS, dtype=jnp.float32)
    pre = low_back(matmul(latent, w_lat) + matmul(onehot, w_act))
    state = jax.nn.relu(layer_norm(pre, gain_input))
    inner = low(jax.nn.relu(layer_norm(state, gain_block)))
    hidden = low(jax.nn.relu(low_back(matmul(inner, w_one))))
    out = state + low_back(matmul(hidden, w_two))
    head = low(layer_norm(out, gain_head))
    logit_c = low_back(matmul(head, w_chance))
    logit_v = low_back(matmul(head, w_value))
    code_hot = jax.nn.one_hot(codes, CODES, dtype=jnp.float32)
    cross_c = jax.nn.logsumexp(logit_c, axis=1) - lax.optimization_barrier(jnp.sum(code_hot * logit_c, axis=1))
    cross_v = jax.nn.logsumexp(logit_v, axis=1) - lax.optimization_barrier(jnp.sum(target * logit_v, axis=1))
    return jnp.sum(weight * (cross_c + cross_v))

def reference(latent, future_latent, actions, codes, lengths, w_lat, w_act, gain_input, gain_block, w_one, w_two, gain_head, w_chance, w_value, w_target):
    blocks = N_GRP * N_BATCH
    per_block = ROWS // blocks
    half = ROWS // 2
    moved = jnp.concatenate([future_latent[half:], future_latent[:half]], axis=0).reshape(blocks, per_block, D)
    table = w_target.astype(jnp.float32)
    target = lax.map(lambda piece: low(jax.nn.softmax(matmul(piece.astype(jnp.float32), table), axis=1)), moved)
    steps_idx = jnp.arange(UNROLL, dtype=jnp.int32)
    mask = (steps_idx[None, :] < lengths[:, None]).astype(jnp.float32).reshape(blocks, per_block)
    weight = mask / jnp.sqrt(jnp.float32(TRAJ))
    acts = actions.reshape(blocks, per_block)
    code_rows = codes.reshape(blocks, per_block)
    params = (w_lat.astype(jnp.float32), w_act.astype(jnp.float32), gain_input, gain_block, w_one.astype(jnp.float32), w_two.astype(jnp.float32), gain_head, w_chance.astype(jnp.float32), w_value.astype(jnp.float32))
    stepped = jax.checkpoint(block_loss)

    def total(params, latent_full):

        def one_block(carry, pieces):
            lat, act, code, targ, wgt = pieces
            return (carry + stepped(params, lat, act, code, targ, wgt), None)
        summed, _ = lax.scan(one_block, jnp.zeros((), jnp.float32), (latent_full.reshape(blocks, per_block, D), acts, code_rows, target, weight))
        return summed
    loss_value, pull = jax.vjp(total, params, latent.astype(jnp.float32))
    grads, grad_latent = pull(jnp.ones((), loss_value.dtype))
    return (grad_latent, grads[0], grads[1], grads[2], grads[3], grads[4], grads[5], grads[6], grads[7], grads[8])
```

```python
import functools
import math

import jax
import jax.numpy as jnp
from jax import lax
from jax.experimental import pallas as pl
from jax.experimental.pallas import tpu as pltpu
from jax.sharding import PartitionSpec as P

D = 256
ACTIONS = 4
CODES = 32
BINS = 601
UNROLL = 5
EPSILON = 1e-05
WIDE = 640
CODE_AT = WIDE - CODES
ROWS = 1280
F32 = jnp.float32
BF16 = jnp.bfloat16

AT_HEAD = 0
AT_TWO = 640
AT_ONE = 896
AT_LAT = 1152
AT_ACT = 1408
AT_GAIN = 1424
PACKED = 1536


def dot(left, right, over_left, over_right):
    return lax.dot_general(
        left,
        right,
        (((over_left,), (over_right,)), ((), ())),
        preferred_element_type=F32,
    )


def norm_forward(value, gain):
    center = value - jnp.mean(value, axis=1, keepdims=True)
    scaled = lax.rsqrt(jnp.mean(center * center, axis=1, keepdims=True) + EPSILON)
    normed = center * scaled
    return normed * gain, normed, scaled


def norm_backward(grad, gain, normed, scaled):
    gained = grad * gain
    along = grad * normed
    gain_grad = jnp.sum(along.reshape(-1, 8, D), axis=0)
    centered = (
        gained
        - jnp.mean(gained, axis=1, keepdims=True)
        - normed * jnp.mean(along * gain, axis=1, keepdims=True)
    )
    return scaled * centered, gain_grad


def pieces(value):
    return [value[:, at : at + 128] for at in range(0, WIDE, 128)]


def exps_and_sum(logits):
    top = jnp.max(functools.reduce(jnp.maximum, logits), axis=1, keepdims=True)
    exps = [jnp.exp(piece - top) for piece in logits]
    return exps, jnp.sum(functools.reduce(jnp.add, exps), axis=1, keepdims=True)


def tower(scale, first, *refs):
    (latent_ref, moved_ref, index_ref, w_lat, w_act, gain_in, gain_bl, gain_he) = refs[:8]
    (w_one, w_two, w_chance, w_value, w_target) = refs[8:13]
    if first:
        grad_latent, packed, heads, encoder, acts, picks = refs[13:]
    else:
        before, _, grad_latent, packed, heads, encoder, acts, picks = refs[13:]
    rows = latent_ref.shape[0]

    @pl.when(pl.program_id(0) == 0)
    def _():
        gap = jnp.zeros((D, CODE_AT - BINS), F32)
        heads[...] = jnp.concatenate(
            [w_value[...].astype(F32), gap, w_chance[...].astype(F32)], axis=1
        ).astype(BF16)
        encoder[...] = jnp.concatenate(
            [w_target[...].astype(F32), jnp.zeros((D, WIDE - BINS), F32)], axis=1
        ).astype(BF16)
        acts[...] = jnp.concatenate(
            [w_act[...].astype(F32), jnp.zeros((16 - ACTIONS, D), F32)], axis=0
        ).astype(BF16)
        row = lax.broadcasted_iota(jnp.int32, (48, D), 0)
        col = lax.broadcasted_iota(jnp.int32, (48, D), 1)
        coded = (row < CODES) & (col == row + 128 - CODES)
        picks[...] = jnp.where(coded | ((row == CODES) & (col >= 128)), 1.0, 0.0).astype(BF16)
        packed[...] = jnp.zeros_like(packed) if first else before[...]

    lane = lax.broadcasted_iota(jnp.int32, (1, 128), 1)
    hide_value = jnp.where(lane < BINS - (WIDE - 128), 0.0, -1e30)
    hide_code = jnp.where(lane >= 128 - CODES, 0.0, -1e30)
    index = index_ref[...].reshape(3, rows)
    act_hot = (lax.broadcasted_iota(jnp.int32, (16, rows), 0) == index[0:1]).astype(F32)
    act_hot = act_hot.astype(BF16)
    kind = lax.broadcasted_iota(jnp.int32, (48, rows), 0)
    row_facts = jnp.where(
        kind == CODES, index[2:3].astype(F32), (kind == index[1:2]).astype(F32)
    ).astype(BF16)

    latent = latent_ref[...]
    pre = dot(latent, w_lat[...], 1, 0) + dot(act_hot, acts[...], 0, 0)
    first_out, first_norm, first_scale = norm_forward(pre, gain_in[...])
    state = jnp.maximum(first_out, 0.0)
    second_out, second_norm, second_scale = norm_forward(state, gain_bl[...])
    inner = jnp.maximum(second_out, 0.0).astype(BF16)
    hidden = jnp.maximum(dot(inner, w_one[...], 1, 0), 0.0).astype(BF16)
    out = state + dot(hidden, w_two[...], 1, 0)
    head_out, head_norm, head_scale = norm_forward(out, gain_he[...])
    head = head_out.astype(BF16)

    facts = dot(row_facts, picks[...], 0, 0)
    code_hot = facts[:, :128]
    weight = facts[:, 128:] * scale

    logits = pieces(dot(moved_ref[...], encoder[...], 1, 0))
    exps, total = exps_and_sum(logits[:4] + [logits[4] + hide_value])
    share = 1.0 / total
    target = [(e * share).astype(BF16).astype(F32) for e in exps]

    logits = pieces(dot(head, heads[...], 1, 0))
    exps, total = exps_and_sum(logits[:4] + [logits[4] + hide_value])
    share = 1.0 / total
    code_exps, code_total = exps_and_sum([logits[4] + hide_code])
    grads = [e * share - t for e, t in zip(exps, target)]
    grads[4] = grads[4] + (code_exps[0] * (1.0 / code_total) - code_hot)
    grad_logits = jnp.concatenate([(g * weight).astype(BF16) for g in grads], axis=1)

    grad_heads = dot(head, grad_logits, 0, 0)
    packed[0:256, :] += grad_heads[:, 0:256]
    packed[256:512, :] += grad_heads[:, 256:512]
    packed[512:640, 0:128] += grad_heads[0:128, 512:640]
    packed[512:640, 128:256] += grad_heads[128:256, 512:640]
    grad_head = dot(grad_logits, heads[...], 1, 1)

    grad_out, gain = norm_backward(grad_head, gain_he[...], head_norm, head_scale)
    packed[AT_GAIN + 16 : AT_GAIN + 24, :] += gain
    grad_branch = grad_out.astype(BF16)
    packed[AT_TWO : AT_TWO + 256, :] += dot(hidden, grad_branch, 0, 0)
    grad_zed = jnp.where(
        hidden > 0, dot(grad_branch, w_two[...], 1, 1).astype(BF16), jnp.zeros((), BF16)
    )
    packed[AT_ONE : AT_ONE + 256, :] += dot(inner, grad_zed, 0, 0)
    grad_second = jnp.where(second_out > 0, dot(grad_zed, w_one[...], 1, 1), 0.0)
    through, gain = norm_backward(grad_second, gain_bl[...], second_norm, second_scale)
    packed[AT_GAIN + 8 : AT_GAIN + 16, :] += gain
    grad_first = jnp.where(first_out > 0, grad_out + through, 0.0)
    grad_pre, gain = norm_backward(grad_first, gain_in[...], first_norm, first_scale)
    packed[AT_GAIN : AT_GAIN + 8, :] += gain
    grad_pre = grad_pre.astype(BF16)
    packed[AT_LAT : AT_LAT + 256, :] += dot(latent, grad_pre, 0, 0)
    packed[AT_ACT : AT_ACT + 16, :] += dot(act_hot, grad_pre, 1, 0)
    grad_latent[...] = dot(grad_pre, w_lat[...], 1, 1)


def run_tower(scale, at, steps, latent, moved, index, weights, before):
    rows = latent.shape[0]

    def whole(array):
        zeros = (0,) * array.ndim
        return pl.BlockSpec(array.shape, lambda i: zeros)

    def blocks(start):
        return pl.BlockSpec((ROWS, D), lambda i: (i + start, 0))

    first = before is None
    in_specs = [blocks(at), blocks(0), pl.BlockSpec((3, 1, ROWS), lambda i: (0, 0, i + at))]
    in_specs += [whole(w) for w in weights]
    args = [latent, moved, index, *weights]
    aliases = {}
    if not first:
        in_specs += [pl.BlockSpec((PACKED, D), lambda i: (0, 0)), pl.BlockSpec(memory_space=pl.ANY)]
        args += [before[1], before[0]]
        aliases = {len(args) - 1: 0}
    return pl.pallas_call(
        functools.partial(tower, scale, first),
        grid=(steps,),
        in_specs=in_specs,
        out_specs=[blocks(at), pl.BlockSpec((PACKED, D), lambda i: (0, 0))],
        out_shape=[
            jax.ShapeDtypeStruct((rows, D), F32),
            jax.ShapeDtypeStruct((PACKED, D), F32),
        ],
        scratch_shapes=[
            pltpu.VMEM((D, WIDE), BF16),
            pltpu.VMEM((D, WIDE), BF16),
            pltpu.VMEM((16, D), BF16),
            pltpu.VMEM((48, D), BF16),
        ],
        input_output_aliases=aliases,
        compiler_params=pltpu.CompilerParams(vmem_limit_bytes=60 << 20),
        cost_estimate=pl.CostEstimate(
            flops=steps * ROWS * 2500000,
            bytes_accessed=steps * ROWS * 2048,
            transcendentals=steps * ROWS * 1280,
        ),
        name="tower",
    )(*args)


def sum_over_all(packed):
    rows = packed.shape[0] // 2
    core = lax.axis_index("grp")
    count = lax.axis_size("batch")
    swap = [(0, 1), (1, 0)]
    low, high = packed[:rows], packed[rows:]
    keep = jnp.where(core == 0, low, high)
    other = jnp.where(core == 0, high, low)
    mine = keep + lax.ppermute(other, "grp", swap)
    share = lax.all_to_all(mine.reshape(count, -1, D), "batch", 0, 0, tiled=True)
    share = jnp.sum(share, axis=0)
    mine = jnp.broadcast_to(share[None], (count, *share.shape))
    mine = lax.all_to_all(mine, "batch", 0, 0, tiled=True).reshape(rows, D)
    other = lax.ppermute(mine, "grp", swap)
    low = jnp.where(core == 0, mine, other)
    high = jnp.where(core == 0, other, mine)
    return jnp.concatenate([low, high], axis=0)


def body(
    latent,
    future_latent,
    actions,
    codes,
    lengths,
    w_lat,
    w_act,
    gain_input,
    gain_block,
    w_one,
    w_two,
    gain_head,
    w_chance,
    w_value,
    w_target,
):
    rows = latent.shape[0]
    swap = [(0, 1), (1, 0)]
    moved_a = lax.ppermute(future_latent[:ROWS], "grp", swap)
    moved_b = lax.ppermute(future_latent[ROWS:], "grp", swap)
    traj_total = lengths.shape[0] * lax.axis_size("grp") * lax.axis_size("batch")
    steps_idx = jnp.arange(UNROLL, dtype=jnp.int32)
    mask = (steps_idx[None, :] < lengths[:, None]).astype(jnp.int32).reshape(-1)
    index = jnp.stack([actions, codes, mask])[:, None, :]
    weights = (
        w_lat,
        w_act,
        gain_input[None],
        gain_block[None],
        gain_head[None],
        w_one,
        w_two,
        w_chance,
        w_value,
        w_target,
    )
    scale = 1.0 / math.sqrt(traj_total)
    part = run_tower(scale, 0, 1, latent, moved_a, index, weights, None)
    grad_latent, packed = run_tower(
        scale, 1, rows // ROWS - 1, latent, moved_b, index, weights, part
    )
    packed = sum_over_all(packed)
    tail = packed[512:640].reshape(128, 2, 128).transpose(1, 0, 2).reshape(D, 128)
    grad_w_value = jnp.concatenate(
        [packed[0:256], packed[256:512], tail[:, : BINS - 512]], axis=1
    )
    gains = jnp.sum(packed[AT_GAIN : AT_GAIN + 24].reshape(3, 8, D), axis=1)
    return (
        grad_latent,
        packed[AT_LAT : AT_LAT + 256],
        packed[AT_ACT : AT_ACT + ACTIONS],
        gains[0],
        gains[1],
        packed[AT_ONE : AT_ONE + 256],
        packed[AT_TWO : AT_TWO + 256],
        gains[2],
        tail[:, 128 - CODES :],
        grad_w_value,
    )


def solution(mesh):
    split = P(("grp", "batch"))
    rows = P(("grp", "batch"), None)
    in_specs = (rows, rows, split, split, split) + (P(),) * 10
    out_specs = (rows,) + (P(),) * 9
    return jax.shard_map(body, mesh=mesh, in_specs=in_specs, out_specs=out_specs, check_vma=False)
```

```python
import functools
import math

import jax
import jax.numpy as jnp
from jax import lax
from jax.experimental import pallas as pl
from jax.experimental.pallas import tpu as pltpu
from jax.sharding import PartitionSpec as P

D = 256
ACTIONS = 4
CODES = 32
BINS = 601
UNROLL = 5
EPSILON = 1e-05
WIDE = 640
CODE_AT = WIDE - CODES
ROWS = 1280
F32 = jnp.float32
BF16 = jnp.bfloat16

AT_TWO = 640
AT_ONE = 896
AT_LAT = 1152
AT_ACT = 1408
AT_GAIN = 1424
PACKED = 1536
HALF = PACKED // 2
RUN_TWO = 0
RUN_ONE = 256
RUN_LAT = 512
RUN_ACT = 768
RUN_GAIN = 784
RUNNING = 808


def dot(left, right, over_left, over_right):
    return lax.dot_general(
        left,
        right,
        (((over_left,), (over_right,)), ((), ())),
        preferred_element_type=F32,
    )


def norm_forward(value, gain):
    center = value - jnp.mean(value, axis=1, keepdims=True)
    scaled = lax.rsqrt(jnp.mean(center * center, axis=1, keepdims=True) + EPSILON)
    normed = center * scaled
    return normed * gain, normed, scaled


def norm_backward(grad, gain, normed, scaled):
    gained = grad * gain
    along = grad * normed
    gain_grad = jnp.sum(along.reshape(-1, 8, D), axis=0)
    centered = (
        gained
        - jnp.mean(gained, axis=1, keepdims=True)
        - normed * jnp.mean(along * gain, axis=1, keepdims=True)
    )
    return scaled * centered, gain_grad


def pieces(value):
    return [value[:, at : at + 128] for at in range(0, WIDE, 128)]


def exps_and_sum(logits):
    top = jnp.max(functools.reduce(jnp.maximum, logits), axis=1, keepdims=True)
    exps = [jnp.exp(piece - top) for piece in logits]
    return exps, jnp.sum(functools.reduce(jnp.add, exps), axis=1, keepdims=True)


def tower(scale, first, *refs):
    (core, latent_ref, moved_ref, index_ref, w_lat, w_act, gain_in, gain_bl, gain_he) = refs[:9]
    (w_one, w_two, w_chance, w_value, w_target) = refs[9:14]
    if first:
        grad_latent, head_sums, sums, heads, encoder, acts, picks = refs[14:]
    else:
        head_before, before, _, grad_latent, stay, send = refs[14:20]
        heads, encoder, acts, picks, head_sums, sums, packed = refs[20:]
    rows = latent_ref.shape[0]

    @pl.when(pl.program_id(0) == 0)
    def _():
        gap = jnp.zeros((CODE_AT - BINS, D), F32)
        heads[...] = jnp.concatenate(
            [w_value[...].astype(F32), gap, w_chance[...].astype(F32)], axis=0
        ).astype(BF16)
        encoder[...] = jnp.concatenate(
            [w_target[...].astype(F32), jnp.zeros((WIDE - BINS, D), F32)], axis=0
        ).astype(BF16)
        acts[...] = jnp.concatenate(
            [w_act[...].astype(F32), jnp.zeros((16 - ACTIONS, D), F32)], axis=0
        ).astype(BF16)
        row = lax.broadcasted_iota(jnp.int32, (48, D), 0)
        col = lax.broadcasted_iota(jnp.int32, (48, D), 1)
        coded = (row < CODES) & (col == row + 128 - CODES)
        picks[...] = jnp.where(coded | ((row == CODES) & (col >= 128)), 1.0, 0.0).astype(BF16)
        head_sums[...] = jnp.zeros_like(head_sums) if first else head_before[...]
        sums[...] = jnp.zeros_like(sums) if first else before[...]

    lane = lax.broadcasted_iota(jnp.int32, (1, 128), 1)
    hide_value = jnp.where(lane < BINS - (WIDE - 128), 0.0, -1e30)
    hide_code = jnp.where(lane >= 128 - CODES, 0.0, -1e30)
    index = index_ref[...].reshape(3, rows)
    act_hot = (lax.broadcasted_iota(jnp.int32, (16, rows), 0) == index[0:1]).astype(F32)
    act_hot = act_hot.astype(BF16)
    kind = lax.broadcasted_iota(jnp.int32, (48, rows), 0)
    row_facts = jnp.where(
        kind == CODES, index[2:3].astype(F32), (kind == index[1:2]).astype(F32)
    ).astype(BF16)

    latent = latent_ref[...]
    pre = dot(latent, w_lat[...], 1, 0) + dot(act_hot, acts[...], 0, 0)
    first_out, first_norm, first_scale = norm_forward(pre, gain_in[...])
    state = jnp.maximum(first_out, 0.0)
    second_out, second_norm, second_scale = norm_forward(state, gain_bl[...])
    inner = jnp.maximum(second_out, 0.0).astype(BF16)
    hidden = jnp.maximum(dot(inner, w_one[...], 1, 0), 0.0).astype(BF16)
    out = state + dot(hidden, w_two[...], 1, 0)
    head_out, head_norm, head_scale = norm_forward(out, gain_he[...])
    head = head_out.astype(BF16)

    facts = dot(row_facts, picks[...], 0, 0)
    code_hot = facts[:, :128]
    weight = facts[:, 128:] * scale

    logits = pieces(dot(moved_ref[...], encoder[...], 1, 1))
    exps, total = exps_and_sum(logits[:4] + [logits[4] + hide_value])
    share = 1.0 / total
    target = [(e * share).astype(BF16).astype(F32) for e in exps]

    logits = pieces(dot(head, heads[...], 1, 1))
    exps, total = exps_and_sum(logits[:4] + [logits[4] + hide_value])
    share = 1.0 / total
    code_exps, code_total = exps_and_sum([logits[4] + hide_code])
    grads = [e * share - t for e, t in zip(exps, target)]
    grads[4] = grads[4] + (code_exps[0] * (1.0 / code_total) - code_hot)
    grad_logits = jnp.concatenate([(g * weight).astype(BF16) for g in grads], axis=1)

    head_sums[...] += dot(head, grad_logits, 0, 0)
    grad_head = dot(grad_logits, heads[...], 1, 0)

    grad_out, gain = norm_backward(grad_head, gain_he[...], head_norm, head_scale)
    sums[RUN_GAIN + 16 : RUN_GAIN + 24, :] += gain
    grad_branch = grad_out.astype(BF16)
    sums[RUN_TWO : RUN_TWO + 256, :] += dot(hidden, grad_branch, 0, 0)
    grad_zed = jnp.where(
        hidden > 0, dot(grad_branch, w_two[...], 1, 1).astype(BF16), jnp.zeros((), BF16)
    )
    sums[RUN_ONE : RUN_ONE + 256, :] += dot(inner, grad_zed, 0, 0)
    grad_second = jnp.where(second_out > 0, dot(grad_zed, w_one[...], 1, 1), 0.0)
    through, gain = norm_backward(grad_second, gain_bl[...], second_norm, second_scale)
    sums[RUN_GAIN + 8 : RUN_GAIN + 16, :] += gain
    grad_first = jnp.where(first_out > 0, grad_out + through, 0.0)
    grad_pre, gain = norm_backward(grad_first, gain_in[...], first_norm, first_scale)
    sums[RUN_GAIN : RUN_GAIN + 8, :] += gain
    grad_pre = grad_pre.astype(BF16)
    sums[RUN_LAT : RUN_LAT + 256, :] += dot(latent, grad_pre, 0, 0)
    sums[RUN_ACT : RUN_ACT + 16, :] += dot(act_hot, grad_pre, 1, 0)
    grad_latent[...] = dot(grad_pre, w_lat[...], 1, 1)


    if not first:

        @pl.when(pl.program_id(0) == pl.num_programs(0) - 1)
        def _():
            packed[0:WIDE, :] = head_sums[...].T
            packed[AT_TWO:AT_GAIN, :] = sums[0:RUN_GAIN, :]
            gains = [
                jnp.sum(sums[RUN_GAIN + at : RUN_GAIN + at + 8, :], axis=0, keepdims=True)
                for at in (0, 8, 16)
            ]
            gains.append(jnp.zeros((PACKED - AT_GAIN - 3, D), F32))
            packed[AT_GAIN:, :] = jnp.concatenate(gains, axis=0)
            mine = pl.multiple_of(core[0] * HALF, HALF)
            stay[...] = packed[pl.ds(mine, HALF), :]
            send[...] = packed[pl.ds(HALF - mine, HALF), :].astype(BF16)


def unpack(core, mine, other, lat, act, gain_in, gain_bl, one, two, gain_he, chance, value, packed):
    at = pl.multiple_of(core[0] * HALF, HALF)
    packed[pl.ds(at, HALF), :] = mine[...].astype(F32)
    packed[pl.ds(HALF - at, HALF), :] = other[...].astype(F32)
    value[...] = packed[0:BINS, :]
    chance[...] = packed[CODE_AT:WIDE, :]
    two[...] = packed[AT_TWO : AT_TWO + D, :]
    one[...] = packed[AT_ONE : AT_ONE + D, :]
    lat[...] = packed[AT_LAT : AT_LAT + D, :]
    act[...] = packed[AT_ACT : AT_ACT + ACTIONS, :]
    gain_in[...] = packed[AT_GAIN : AT_GAIN + 1, :]
    gain_bl[...] = packed[AT_GAIN + 1 : AT_GAIN + 2, :]
    gain_he[...] = packed[AT_GAIN + 2 : AT_GAIN + 3, :]


def run_tower(scale, core, at, steps, latent, moved, index, weights, before):
    rows = latent.shape[0]

    def whole(array):
        zeros = (0,) * array.ndim
        return pl.BlockSpec(array.shape, lambda i: zeros)

    def shape(rows, cols, kind=F32):
        return jax.ShapeDtypeStruct((rows, cols), kind)

    blocks = pl.BlockSpec((ROWS, D), lambda i: (i + at, 0))
    first = before is None
    in_specs = [pl.BlockSpec(memory_space=pltpu.SMEM), blocks, blocks]
    in_specs += [pl.BlockSpec((3, 1, ROWS), lambda i: (0, 0, i + at))]
    in_specs += [whole(w) for w in weights]
    args = [core, latent, moved, index, *weights]
    scratch = [
        pltpu.VMEM((WIDE, D), BF16),
        pltpu.VMEM((WIDE, D), BF16),
        pltpu.VMEM((16, D), BF16),
        pltpu.VMEM((48, D), BF16),
    ]
    aliases = {}
    if first:
        results = [shape(D, WIDE), shape(RUNNING, D)]
    else:
        results = [shape(HALF, D), shape(HALF, D, BF16)]
        scratch += [pltpu.VMEM((D, WIDE), F32), pltpu.VMEM((RUNNING, D), F32)]
        scratch += [pltpu.VMEM((PACKED, D), F32)]
        in_specs += [whole(before[1]), whole(before[2]), pl.BlockSpec(memory_space=pl.ANY)]
        args += [before[1], before[2], before[0]]
        aliases = {len(args) - 1: 0}
    return pl.pallas_call(
        functools.partial(tower, scale, first),
        grid=(steps,),
        in_specs=in_specs,
        out_specs=[blocks] + [whole(r) for r in results],
        out_shape=[shape(rows, D)] + results,
        scratch_shapes=scratch,
        input_output_aliases=aliases,
        compiler_params=pltpu.CompilerParams(vmem_limit_bytes=60 << 20),
        cost_estimate=pl.CostEstimate(
            flops=steps * ROWS * 2500000,
            bytes_accessed=steps * ROWS * 2048,
            transcendentals=steps * ROWS * 1280,
        ),
        name="tower",
    )(*args)


def sum_over_chips(mine):
    count = lax.axis_size("batch")
    near = 8 if count == 16 else count
    groups = [[at * near + i for i in range(near)] for at in range(count // near)]
    swap = functools.partial(
        lax.all_to_all,
        axis_name="batch",
        split_axis=0,
        concat_axis=0,
        tiled=True,
        axis_index_groups=groups,
    )
    rows = mine.shape[0]
    share = swap(mine.reshape(near, -1, D))
    share = jnp.sum(share.astype(F32), axis=0).astype(BF16)
    if count == 2 * near:
        far = lax.ppermute(share, "batch", [(i, (i + near) % count) for i in range(count)])
        share = (share.astype(F32) + far.astype(F32)).astype(BF16)
    return swap(jnp.broadcast_to(share[None], (near, *share.shape))).reshape(rows, D)


def finish(core, stay, send):
    swap = [(0, 1), (1, 0)]
    mine = (stay + lax.ppermute(send, "grp", swap).astype(F32)).astype(BF16)
    mine = sum_over_chips(mine)
    other = lax.ppermute(mine, "grp", swap)
    sizes = (D, ACTIONS, 1, 1, D, D, 1, CODES, BINS)
    return pl.pallas_call(
        unpack,
        in_specs=[pl.BlockSpec(memory_space=pltpu.SMEM)] + [pl.BlockSpec(memory_space=pltpu.VMEM)] * 2,
        out_shape=[jax.ShapeDtypeStruct((n, D), F32) for n in sizes],
        scratch_shapes=[pltpu.VMEM((PACKED, D), F32)],
        name="unpack",
    )(core, mine, other)


def body(
    latent,
    future_latent,
    actions,
    codes,
    lengths,
    w_lat,
    w_act,
    gain_input,
    gain_block,
    w_one,
    w_two,
    gain_head,
    w_chance,
    w_value,
    w_target,
):
    rows = latent.shape[0]
    swap = [(0, 1), (1, 0)]
    moved_a = lax.ppermute(future_latent[:ROWS], "grp", swap)
    moved_b = lax.ppermute(future_latent, "grp", swap)
    traj_total = lengths.shape[0] * lax.axis_size("grp") * lax.axis_size("batch")
    steps_idx = jnp.arange(UNROLL, dtype=jnp.int32)
    mask = (steps_idx[None, :] < lengths[:, None]).astype(jnp.int32).reshape(-1)
    index = jnp.stack([actions, codes, mask])[:, None, :]
    weights = (
        w_lat,
        w_act,
        gain_input[None],
        gain_block[None],
        gain_head[None],
        w_one,
        w_two,
        w_chance.T,
        w_value.T,
        w_target.T,
    )
    scale = 1.0 / math.sqrt(traj_total)
    core = lax.axis_index("grp").astype(jnp.int32).reshape(1)
    part = run_tower(scale, core, 0, 1, latent, moved_a, index, weights, None)
    grad_latent, stay, send = run_tower(
        scale, core, 1, rows // ROWS - 1, latent, moved_b, index, weights, part
    )
    lat, act, gain_in, gain_bl, one, two, gain_he, chance, value = finish(core, stay, send)
    return (
        grad_latent,
        lat,
        act,
        gain_in[0],
        gain_bl[0],
        one,
        two,
        gain_he[0],
        chance.T,
        value.T,
    )


def solution(mesh):
    split = P(("grp", "batch"))
    rows = P(("grp", "batch"), None)
    in_specs = (rows, rows, split, split, split) + (P(),) * 10
    out_specs = (rows,) + (P(),) * 9
    return jax.shard_map(body, mesh=mesh, in_specs=in_specs, out_specs=out_specs, check_vma=False)
```

```python
import functools
import math

import jax
import jax.numpy as jnp
from jax import lax
from jax.experimental import pallas as pl
from jax.experimental.pallas import tpu as pltpu
from jax.sharding import PartitionSpec as P

D = 256
ACTIONS = 4
CODES = 32
BINS = 601
UNROLL = 5
EPSILON = 1e-05
WIDE = 640
CODE_AT = WIDE - CODES
ROWS = 1280
SUB = 640
LAG = 6
F32 = jnp.float32
BF16 = jnp.bfloat16

AT_TWO = 640
AT_ONE = 896
AT_LAT = 1152
AT_ACT = 1408
AT_GAIN = 1424
PACKED = 1536
HALF = PACKED // 2
RUN_TWO = 0
RUN_ONE = 256
RUN_LAT = 512
RUN_ACT = 768
RUN_GAIN = 784
RUNNING = 808


def dot(left, right, over_left, over_right):
    return lax.dot_general(
        left,
        right,
        (((over_left,), (over_right,)), ((), ())),
        preferred_element_type=F32,
    )


def normalize(value):
    center = value - jnp.mean(value, axis=1, keepdims=True)
    scaled = lax.rsqrt(jnp.mean(center * center, axis=1, keepdims=True) + EPSILON)
    return center * scaled, scaled


def norm_backward(grad, gain, normed, scaled):
    gained = grad * gain
    along = gained * normed
    centered = (
        gained
        - jnp.mean(gained, axis=1, keepdims=True)
        - normed * jnp.mean(along, axis=1, keepdims=True)
    )
    return scaled * centered, jnp.sum(along.reshape(-1, 8, D), axis=0)


def add_up(parts):
    return jnp.sum(parts.reshape(-1, 8, D), axis=0)


def pieces(value):
    return [value[:, at : at + 128] for at in range(0, WIDE, 128)]


def exps_and_sum(logits):
    top = jnp.max(functools.reduce(jnp.maximum, logits), axis=1, keepdims=True)
    exps = [jnp.exp(piece - top) for piece in logits]
    return exps, jnp.sum(functools.reduce(jnp.add, exps), axis=1, keepdims=True)


def tower(scale, first, *refs):
    (core, latent_ref, moved_ref, index_ref, w_lat, w_act, gain_in, gain_bl, gain_he) = refs[:9]
    (w_one, w_two, w_chance, w_value, w_target) = refs[9:14]
    if first:
        grad_latent, head_sums, sums, heads, encoder, acts, picks = refs[14:]
    else:
        head_before, before, _, grad_latent, stay, send = refs[14:20]
        heads, encoder, acts, picks, head_sums, sums, packed = refs[20:]
    rows = latent_ref.shape[0]

    @pl.when(pl.program_id(0) == 0)
    def _():
        gap = jnp.zeros((CODE_AT - BINS, D), F32)
        heads[...] = jnp.concatenate(
            [w_value[...].astype(F32), gap, w_chance[...].astype(F32)], axis=0
        ).astype(BF16)
        encoder[...] = jnp.concatenate(
            [w_target[...].astype(F32), jnp.zeros((WIDE - BINS, D), F32)], axis=0
        ).astype(BF16)
        acts[...] = jnp.concatenate(
            [w_act[...].astype(F32), jnp.zeros((16 - ACTIONS, D), F32)], axis=0
        ).astype(BF16)
        row = lax.broadcasted_iota(jnp.int32, (48, D), 0)
        col = lax.broadcasted_iota(jnp.int32, (48, D), 1)
        coded = (row < CODES) & (col == row + 128 - CODES)
        picks[...] = jnp.where(coded | ((row == CODES) & (col >= 128)), 1.0, 0.0).astype(BF16)
        head_sums[...] = jnp.zeros_like(head_sums) if first else head_before[...]
        sums[...] = jnp.zeros_like(sums) if first else before[...]

    lane = lax.broadcasted_iota(jnp.int32, (1, 128), 1)
    hide_value = jnp.where(lane < BINS - (WIDE - 128), 0.0, -1e30)
    hide_code = jnp.where(lane >= 128 - CODES, 0.0, -1e30)

    def one_part(at):
        span = slice(at, at + SUB)
        index = index_ref[:, :, span].reshape(3, SUB)
        act_hot = (lax.broadcasted_iota(jnp.int32, (16, SUB), 0) == index[0:1]).astype(F32)
        act_hot = act_hot.astype(BF16)
        kind = lax.broadcasted_iota(jnp.int32, (48, SUB), 0)
        row_facts = jnp.where(
            kind == CODES, index[2:3].astype(F32), (kind == index[1:2]).astype(F32)
        ).astype(BF16)

        latent = latent_ref[span, :]
        def first_norm_step(pre):
            normed, scaled = normalize(pre)
            return normed, scaled, jnp.maximum(normed * gain_in[...], 0.0)

        def second_norm_step(state):
            normed, scaled = normalize(state)
            return normed, scaled, jnp.maximum(normed * gain_bl[...], 0.0).astype(BF16)

        def head_norm_step(state, branch):
            normed, scaled = normalize(state + branch)
            return normed, scaled, (normed * gain_he[...]).astype(BF16)

        def target_step(logits):
            logits = pieces(logits)
            exps, total = exps_and_sum(logits[:4] + [logits[4] + hide_value])
            share = 1.0 / total
            return (jnp.concatenate([(e * share).astype(BF16) for e in exps], axis=1),)

        def loss_step(logits, target, facts):
            code_hot = facts[:, :128]
            weight = facts[:, 128:] * scale
            target = [t.astype(F32) for t in pieces(target)]
            logits = pieces(logits)
            exps, total = exps_and_sum(logits[:4] + [logits[4] + hide_value])
            share = 1.0 / total
            code_exps, code_total = exps_and_sum([logits[4] + hide_code])
            grads = [e * share - t for e, t in zip(exps, target)]
            grads[4] = grads[4] + (code_exps[0] * (1.0 / code_total) - code_hot)
            return (jnp.concatenate([(g * weight).astype(BF16) for g in grads], axis=1),)

        def head_back_step(grad, normed, scaled):
            grad, along = norm_backward(grad, gain_he[...], normed, scaled)
            return grad, grad.astype(BF16), along

        def zed_back_step(grad, hidden):
            return (jnp.where(hidden > 0, grad.astype(BF16), jnp.zeros((), BF16)),)

        def block_back_step(grad, normed, scaled, state, grad_out):
            grad = jnp.where(normed > 0, grad, 0.0)
            through, along = norm_backward(grad, gain_bl[...], normed, scaled)
            return jnp.where(state > 0, grad_out + through, 0.0), along

        def first_back_step(grad, normed, scaled):
            grad, along = norm_backward(grad, gain_in[...], normed, scaled)
            return grad.astype(BF16), along

        pre = dot(latent, w_lat[...], 1, 0) + dot(act_hot, acts[...], 0, 0)
        yield
        first_norm, first_scale, state = first_norm_step(pre)
        yield
        second_norm, second_scale, inner = second_norm_step(state)
        yield
        hidden = jnp.maximum(dot(inner, w_one[...], 1, 0), 0.0).astype(BF16)
        yield
        branch = dot(hidden, w_two[...], 1, 0)
        yield
        head_norm, head_scale, head = head_norm_step(state, branch)
        yield
        logits = dot(moved_ref[span, :], encoder[...], 1, 1)
        yield
        (target,) = target_step(logits)
        yield
        facts = dot(row_facts, picks[...], 0, 0)
        logits = dot(head, heads[...], 1, 1)
        yield
        (grad_logits,) = loss_step(logits, target, facts)
        yield
        grad_head = dot(grad_logits, heads[...], 1, 0)
        head_sums[...] += dot(head, grad_logits, 0, 0)
        yield
        grad_out, grad_branch, along = head_back_step(grad_head, head_norm, head_scale)
        sums[RUN_GAIN + 16 : RUN_GAIN + 24, :] += add_up(along)
        yield
        (grad_zed,) = zed_back_step(dot(grad_branch, w_two[...], 1, 1), hidden)
        sums[RUN_TWO : RUN_TWO + 256, :] += dot(hidden, grad_branch, 0, 0)
        yield
        grad_inner = dot(grad_zed, w_one[...], 1, 1)
        sums[RUN_ONE : RUN_ONE + 256, :] += dot(inner, grad_zed, 0, 0)
        yield
        grad_first, along = block_back_step(grad_inner, second_norm, second_scale, state, grad_out)
        sums[RUN_GAIN + 8 : RUN_GAIN + 16, :] += add_up(along)
        yield
        grad_pre, along = first_back_step(grad_first, first_norm, first_scale)
        sums[RUN_GAIN : RUN_GAIN + 8, :] += add_up(along)
        yield
        grad_latent[span, :] = dot(grad_pre, w_lat[...], 1, 1)
        sums[RUN_LAT : RUN_LAT + 256, :] += dot(latent, grad_pre, 0, 0)
        sums[RUN_ACT : RUN_ACT + 16, :] += dot(act_hot, grad_pre, 1, 0)

    parts = [one_part(at) for at in range(0, rows, SUB)]
    turn = 0
    while any(parts):
        for at, part in enumerate(parts):
            if part and turn >= LAG * at and next(part, "end") == "end":
                parts[at] = None
        turn += 1

    if not first:

        @pl.when(pl.program_id(0) == pl.num_programs(0) - 1)
        def _():
            packed[0:WIDE, :] = head_sums[...].T
            packed[AT_TWO:AT_GAIN, :] = sums[0:RUN_GAIN, :]
            gains = [
                jnp.sum(sums[RUN_GAIN + at : RUN_GAIN + at + 8, :], axis=0, keepdims=True) / gain[...]
                for at, gain in ((0, gain_in), (8, gain_bl), (16, gain_he))
            ]
            gains.append(jnp.zeros((PACKED - AT_GAIN - 3, D), F32))
            packed[AT_GAIN:, :] = jnp.concatenate(gains, axis=0)
            mine = pl.multiple_of(core[0] * HALF, HALF)
            stay[...] = packed[pl.ds(mine, HALF), :]
            send[...] = packed[pl.ds(HALF - mine, HALF), :].astype(BF16)


def unpack(core, mine, other, lat, act, gain_in, gain_bl, one, two, gain_he, chance, value, packed):
    at = pl.multiple_of(core[0] * HALF, HALF)
    packed[pl.ds(at, HALF), :] = mine[...].astype(F32)
    packed[pl.ds(HALF - at, HALF), :] = other[...].astype(F32)
    value[...] = packed[0:BINS, :]
    chance[...] = packed[CODE_AT:WIDE, :]
    two[...] = packed[AT_TWO : AT_TWO + D, :]
    one[...] = packed[AT_ONE : AT_ONE + D, :]
    lat[...] = packed[AT_LAT : AT_LAT + D, :]
    act[...] = packed[AT_ACT : AT_ACT + ACTIONS, :]
    gain_in[...] = packed[AT_GAIN : AT_GAIN + 1, :]
    gain_bl[...] = packed[AT_GAIN + 1 : AT_GAIN + 2, :]
    gain_he[...] = packed[AT_GAIN + 2 : AT_GAIN + 3, :]


def run_tower(scale, core, at, steps, latent, moved, index, weights, before):
    rows = latent.shape[0]

    def whole(array):
        zeros = (0,) * array.ndim
        return pl.BlockSpec(array.shape, lambda i: zeros)

    def shape(rows, cols, kind=F32):
        return jax.ShapeDtypeStruct((rows, cols), kind)

    blocks = pl.BlockSpec((ROWS, D), lambda i: (i + at, 0))
    first = before is None
    in_specs = [pl.BlockSpec(memory_space=pltpu.SMEM), blocks, blocks]
    in_specs += [pl.BlockSpec((3, 1, ROWS), lambda i: (0, 0, i + at))]
    in_specs += [whole(w) for w in weights]
    args = [core, latent, moved, index, *weights]
    scratch = [
        pltpu.VMEM((WIDE, D), BF16),
        pltpu.VMEM((WIDE, D), BF16),
        pltpu.VMEM((16, D), BF16),
        pltpu.VMEM((48, D), BF16),
    ]
    aliases = {}
    if first:
        results = [shape(D, WIDE), shape(RUNNING, D)]
    else:
        results = [shape(HALF, D), shape(HALF, D, BF16)]
        scratch += [pltpu.VMEM((D, WIDE), F32), pltpu.VMEM((RUNNING, D), F32)]
        scratch += [pltpu.VMEM((PACKED, D), F32)]
        in_specs += [whole(before[1]), whole(before[2]), pl.BlockSpec(memory_space=pl.ANY)]
        args += [before[1], before[2], before[0]]
        aliases = {len(args) - 1: 0}
    return pl.pallas_call(
        functools.partial(tower, scale, first),
        grid=(steps,),
        in_specs=in_specs,
        out_specs=[blocks] + [whole(r) for r in results],
        out_shape=[shape(rows, D)] + results,
        scratch_shapes=scratch,
        input_output_aliases=aliases,
        compiler_params=pltpu.CompilerParams(vmem_limit_bytes=60 << 20),
        cost_estimate=pl.CostEstimate(
            flops=steps * ROWS * 2500000,
            bytes_accessed=steps * ROWS * 2048,
            transcendentals=steps * ROWS * 1280,
        ),
        name="tower",
    )(*args)


def sum_over_chips(mine):
    count = lax.axis_size("batch")
    near = 8 if count == 16 else count
    groups = [[at * near + i for i in range(near)] for at in range(count // near)]
    swap = functools.partial(
        lax.all_to_all,
        axis_name="batch",
        split_axis=0,
        concat_axis=0,
        tiled=True,
        axis_index_groups=groups,
    )
    rows = mine.shape[0]
    share = swap(mine.reshape(near, -1, D))
    share = jnp.sum(share.astype(F32), axis=0).astype(BF16)
    if count == 2 * near:
        far = lax.ppermute(share, "batch", [(i, (i + near) % count) for i in range(count)])
        share = (share.astype(F32) + far.astype(F32)).astype(BF16)
    return swap(jnp.broadcast_to(share[None], (near, *share.shape))).reshape(rows, D)


def finish(core, stay, send):
    swap = [(0, 1), (1, 0)]
    mine = (stay + lax.ppermute(send, "grp", swap).astype(F32)).astype(BF16)
    mine = sum_over_chips(mine)
    other = lax.ppermute(mine, "grp", swap)
    sizes = (D, ACTIONS, 1, 1, D, D, 1, CODES, BINS)
    return pl.pallas_call(
        unpack,
        in_specs=[pl.BlockSpec(memory_space=pltpu.SMEM)] + [pl.BlockSpec(memory_space=pltpu.VMEM)] * 2,
        out_shape=[jax.ShapeDtypeStruct((n, D), F32) for n in sizes],
        scratch_shapes=[pltpu.VMEM((PACKED, D), F32)],
        name="unpack",
    )(core, mine, other)


def body(
    latent,
    future_latent,
    actions,
    codes,
    lengths,
    w_lat,
    w_act,
    gain_input,
    gain_block,
    w_one,
    w_two,
    gain_head,
    w_chance,
    w_value,
    w_target,
):
    rows = latent.shape[0]
    swap = [(0, 1), (1, 0)]
    moved_a = lax.ppermute(future_latent[:ROWS], "grp", swap)
    traj_total = lengths.shape[0] * lax.axis_size("grp") * lax.axis_size("batch")
    steps_idx = jnp.arange(UNROLL, dtype=jnp.int32)
    mask = (steps_idx[None, :] < lengths[:, None]).astype(jnp.int32).reshape(-1)
    index = jnp.stack([actions, codes, mask])[:, None, :]
    moved_a, index, future_latent = lax.optimization_barrier((moved_a, index, future_latent))
    moved_b = lax.ppermute(future_latent, "grp", swap)
    weights = (
        w_lat,
        w_act,
        gain_input[None],
        gain_block[None],
        gain_head[None],
        w_one,
        w_two,
        w_chance.T,
        w_value.T,
        w_target.T,
    )
    scale = 1.0 / math.sqrt(traj_total)
    core = lax.axis_index("grp").astype(jnp.int32).reshape(1)
    part = run_tower(scale, core, 0, 1, latent, moved_a, index, weights, None)
    grad_latent, stay, send = run_tower(
        scale, core, 1, rows // ROWS - 1, latent, moved_b, index, weights, part
    )
    lat, act, gain_in, gain_bl, one, two, gain_he, chance, value = finish(core, stay, send)
    return (
        grad_latent,
        lat,
        act,
        gain_in[0],
        gain_bl[0],
        one,
        two,
        gain_he[0],
        chance.T,
        value.T,
    )


def solution(mesh):
    split = P(("grp", "batch"))
    rows = P(("grp", "batch"), None)
    in_specs = (rows, rows, split, split, split) + (P(),) * 10
    out_specs = (rows,) + (P(),) * 9
    return jax.shard_map(body, mesh=mesh, in_specs=in_specs, out_specs=out_specs, check_vma=False)
```

```python
import functools
import math

import jax
import jax.numpy as jnp
from jax import lax
from jax.experimental import pallas as pl
from jax.experimental.pallas import tpu as pltpu
from jax.sharding import PartitionSpec as P

D = 256
ACTIONS = 4
CODES = 32
BINS = 601
UNROLL = 5
EPSILON = 1e-05
WIDE = 640
CODE_AT = WIDE - CODES
ROWS = 1280
SUB = 640
LAG = 6
STAGES = (
    ("tl",),
    ("pre",),
    ("ln1",),
    ("ln2",),
    ("hid",),
    ("branch",),
    ("lnh",),
    ("tsm",),
    ("lg",),
    ("lsm",),
    ("gh", "hs"),
    ("lbh",),
    ("zed", "two"),
    ("inn", "one"),
    ("lbb",),
    ("lbf",),
    ("lat", "lats"),
)
F32 = jnp.float32
BF16 = jnp.bfloat16

AT_TWO = 640
AT_ONE = 896
AT_LAT = 1152
AT_ACT = 1408
AT_GAIN = 1424
PACKED = 1536
HALF = PACKED // 2
RUN_TWO = 0
RUN_ONE = 256
RUN_LAT = 512
RUN_ACT = 768
RUN_GAIN = 784
RUNNING = 808


def dot(left, right, over_left, over_right):
    return lax.dot_general(
        left,
        right,
        (((over_left,), (over_right,)), ((), ())),
        preferred_element_type=F32,
    )


def normalize(value):
    center = value - jnp.mean(value, axis=1, keepdims=True)
    scaled = lax.rsqrt(jnp.mean(center * center, axis=1, keepdims=True) + EPSILON)
    return center * scaled, scaled


def norm_backward(grad, gain, normed, scaled):
    gained = grad * gain
    along = gained * normed
    centered = (
        gained
        - jnp.mean(gained, axis=1, keepdims=True)
        - normed * jnp.mean(along, axis=1, keepdims=True)
    )
    return scaled * centered, jnp.sum(along.reshape(-1, 8, D), axis=0)


def add_up(parts):
    return jnp.sum(parts.reshape(-1, 8, D), axis=0)


def pieces(value):
    return [value[:, at : at + 128] for at in range(0, WIDE, 128)]


def exps_and_sum(logits):
    top = jnp.max(functools.reduce(jnp.maximum, logits), axis=1, keepdims=True)
    exps = [jnp.exp(piece - top) for piece in logits]
    return exps, jnp.sum(functools.reduce(jnp.add, exps), axis=1, keepdims=True)


def tower(scale, first, *refs):
    (core, latent_ref, moved_ref, action_ref, code_ref, mask_ref) = refs[:6]
    (w_lat, w_act, gain_in, gain_bl, gain_he, w_one, w_two, w_chance, w_value, w_target) = refs[6:16]
    if first:
        grad_latent, head_sums, sums, heads, encoder, acts, picks = refs[16:]
    else:
        head_before, before, _, grad_latent, stay, send = refs[16:22]
        heads, encoder, acts, picks, head_sums, sums, packed = refs[22:]
    rows = latent_ref.shape[0]

    @pl.when(pl.program_id(0) == 0)
    def _():
        gap = jnp.zeros((CODE_AT - BINS, D), F32)
        heads[...] = jnp.concatenate(
            [w_value[...].astype(F32), gap, w_chance[...].astype(F32)], axis=0
        ).astype(BF16)
        encoder[...] = jnp.concatenate(
            [w_target[...].astype(F32), jnp.zeros((WIDE - BINS, D), F32)], axis=0
        ).astype(BF16)
        acts[...] = jnp.concatenate(
            [w_act[...].astype(F32), jnp.zeros((16 - ACTIONS, D), F32)], axis=0
        ).astype(BF16)
        row = lax.broadcasted_iota(jnp.int32, (48, D), 0)
        col = lax.broadcasted_iota(jnp.int32, (48, D), 1)
        coded = (row < CODES) & (col == row + 128 - CODES)
        picks[...] = jnp.where(coded | ((row == CODES) & (col >= 128)), 1.0, 0.0).astype(BF16)
        head_sums[...] = jnp.zeros_like(head_sums) if first else head_before[...]
        sums[...] = jnp.zeros_like(sums) if first else before[...]

    lane = lax.broadcasted_iota(jnp.int32, (1, 128), 1)
    hide_value = jnp.where(lane < BINS - (WIDE - 128), 0.0, -1e30)
    hide_code = jnp.where(lane >= 128 - CODES, 0.0, -1e30)

    def target_step(logits):
        logits = pieces(logits)
        exps, total = exps_and_sum(logits[:4] + [logits[4] + hide_value])
        share = 1.0 / total
        return (jnp.concatenate([(e * share).astype(BF16) for e in exps], axis=1),)

    def one_part(at):
        span = slice(at, at + SUB)
        act_hot = lax.broadcasted_iota(jnp.int32, (16, SUB), 0) == action_ref[:, span]
        act_hot = act_hot.astype(F32).astype(BF16)
        kind = lax.broadcasted_iota(jnp.int32, (48, SUB), 0)
        row_facts = jnp.where(
            kind == CODES, mask_ref[:, span].astype(F32), (kind == code_ref[:, span]).astype(F32)
        ).astype(BF16)

        latent = latent_ref[span, :]
        def first_norm_step(pre):
            normed, scaled = normalize(pre)
            return normed, scaled, jnp.maximum(normed * gain_in[...], 0.0)

        def second_norm_step(state):
            normed, scaled = normalize(state)
            return normed, scaled, jnp.maximum(normed * gain_bl[...], 0.0).astype(BF16)

        def head_norm_step(state, branch):
            normed, scaled = normalize(state + branch)
            return normed, scaled, (normed * gain_he[...]).astype(BF16)

        def loss_step(logits, target, facts):
            code_hot = facts[:, :128]
            weight = facts[:, 128:] * scale
            target = [t.astype(F32) for t in pieces(target)]
            logits = pieces(logits)
            exps, total = exps_and_sum(logits[:4] + [logits[4] + hide_value])
            share = 1.0 / total
            code_exps, code_total = exps_and_sum([logits[4] + hide_code])
            grads = [e * share - t for e, t in zip(exps, target)]
            grads[4] = grads[4] + (code_exps[0] * (1.0 / code_total) - code_hot)
            return (jnp.concatenate([(g * weight).astype(BF16) for g in grads], axis=1),)

        def head_back_step(grad, normed, scaled):
            grad, along = norm_backward(grad, gain_he[...], normed, scaled)
            return grad, grad.astype(BF16), along

        def zed_back_step(grad, hidden):
            return (jnp.where(hidden > 0, grad.astype(BF16), jnp.zeros((), BF16)),)

        def block_back_step(grad, normed, scaled, state, grad_out):
            grad = jnp.where(normed > 0, grad, 0.0)
            through, along = norm_backward(grad, gain_bl[...], normed, scaled)
            return jnp.where(state > 0, grad_out + through, 0.0), along

        def first_back_step(grad, normed, scaled):
            grad, along = norm_backward(grad, gain_in[...], normed, scaled)
            return grad.astype(BF16), along

        pre = dot(latent, w_lat[...], 1, 0) + dot(act_hot, acts[...], 0, 0)
        yield "pre"
        first_norm, first_scale, state = first_norm_step(pre)
        yield "ln1"
        second_norm, second_scale, inner = second_norm_step(state)
        yield "ln2"
        hidden = jnp.maximum(dot(inner, w_one[...], 1, 0), 0.0).astype(BF16)
        yield "hid"
        branch = dot(hidden, w_two[...], 1, 0)
        yield "branch"
        head_norm, head_scale, head = head_norm_step(state, branch)
        yield "lnh"
        facts = dot(row_facts, picks[...], 0, 0)
        logits = dot(head, heads[...], 1, 1)
        yield "lg"
        (grad_logits,) = loss_step(logits, targets[at], facts)
        yield "lsm"
        grad_head = dot(grad_logits, heads[...], 1, 0)
        yield "gh"
        head_sums[...] += dot(head, grad_logits, 0, 0)
        yield "hs"
        grad_out, grad_branch, along = head_back_step(grad_head, head_norm, head_scale)
        sums[RUN_GAIN + 16 : RUN_GAIN + 24, :] += add_up(along)
        yield "lbh"
        (grad_zed,) = zed_back_step(dot(grad_branch, w_two[...], 1, 1), hidden)
        yield "zed"
        sums[RUN_TWO : RUN_TWO + 256, :] += dot(hidden, grad_branch, 0, 0)
        yield "two"
        grad_inner = dot(grad_zed, w_one[...], 1, 1)
        yield "inn"
        sums[RUN_ONE : RUN_ONE + 256, :] += dot(inner, grad_zed, 0, 0)
        yield "one"
        grad_first, along = block_back_step(grad_inner, second_norm, second_scale, state, grad_out)
        sums[RUN_GAIN + 8 : RUN_GAIN + 16, :] += add_up(along)
        yield "lbb"
        grad_pre, along = first_back_step(grad_first, first_norm, first_scale)
        sums[RUN_GAIN : RUN_GAIN + 8, :] += add_up(along)
        yield "lbf"
        grad_latent[span, :] = dot(grad_pre, w_lat[...], 1, 1)
        yield "lat"
        sums[RUN_LAT : RUN_LAT + 256, :] += dot(latent, grad_pre, 0, 0)
        sums[RUN_ACT : RUN_ACT + 16, :] += dot(act_hot, grad_pre, 1, 0)
        yield "lats"

    def one_target(at):
        logits = dot(moved_ref[at : at + SUB, :], encoder[...], 1, 1)
        yield "tl"
        (targets[at],) = target_step(logits)
        yield "tsm"

    targets = {}
    parts = [(one_part(at), one_target(at)) for at in range(0, rows, SUB)]
    for turn in range(len(STAGES) + LAG * (len(parts) - 1)):
        for at, (part, goal) in enumerate(parts):
            if 0 <= turn - LAG * at < len(STAGES):
                for stage in STAGES[turn - LAG * at]:
                    assert next(goal if stage in ("tl", "tsm") else part) == stage

    if not first:

        @pl.when(pl.program_id(0) == pl.num_programs(0) - 1)
        def _():
            packed[0:WIDE, :] = head_sums[...].T
            packed[AT_TWO:AT_GAIN, :] = sums[0:RUN_GAIN, :]
            gains = [
                jnp.sum(sums[RUN_GAIN + at : RUN_GAIN + at + 8, :], axis=0, keepdims=True) / gain[...]
                for at, gain in ((0, gain_in), (8, gain_bl), (16, gain_he))
            ]
            gains.append(jnp.zeros((PACKED - AT_GAIN - 3, D), F32))
            packed[AT_GAIN:, :] = jnp.concatenate(gains, axis=0)
            mine = pl.multiple_of(core[0] * HALF, HALF)
            stay[...] = packed[pl.ds(mine, HALF), :]
            send[...] = packed[pl.ds(HALF - mine, HALF), :].astype(BF16)


def unpack(core, mine, other, lat, act, gain_in, gain_bl, one, two, gain_he, chance, value, packed):
    at = pl.multiple_of(core[0] * HALF, HALF)
    packed[pl.ds(at, HALF), :] = mine[...].astype(F32)
    packed[pl.ds(HALF - at, HALF), :] = other[...].astype(F32)
    value[...] = packed[0:BINS, :]
    chance[...] = packed[CODE_AT:WIDE, :]
    two[...] = packed[AT_TWO : AT_TWO + D, :]
    one[...] = packed[AT_ONE : AT_ONE + D, :]
    lat[...] = packed[AT_LAT : AT_LAT + D, :]
    act[...] = packed[AT_ACT : AT_ACT + ACTIONS, :]
    gain_in[...] = packed[AT_GAIN : AT_GAIN + 1, :]
    gain_bl[...] = packed[AT_GAIN + 1 : AT_GAIN + 2, :]
    gain_he[...] = packed[AT_GAIN + 2 : AT_GAIN + 3, :]


def run_tower(scale, core, at, steps, latent, moved, index, weights, before):
    rows = latent.shape[0]

    def whole(array):
        zeros = (0,) * array.ndim
        return pl.BlockSpec(array.shape, lambda i: zeros)

    def shape(rows, cols, kind=F32):
        return jax.ShapeDtypeStruct((rows, cols), kind)

    blocks = pl.BlockSpec((ROWS, D), lambda i: (i + at, 0))
    first = before is None
    if first:
        moved = pltpu.with_memory_space_constraint(moved, pltpu.VMEM)
        moved_spec = pl.BlockSpec(memory_space=pltpu.VMEM)
    else:
        moved_spec = blocks
    in_specs = [pl.BlockSpec(memory_space=pltpu.SMEM), blocks, moved_spec]
    in_specs += [pl.BlockSpec((1, ROWS), lambda i: (0, i + at))] * 3
    in_specs += [whole(w) for w in weights]
    args = [core, latent, moved, *index, *weights]
    scratch = [
        pltpu.VMEM((WIDE, D), BF16),
        pltpu.VMEM((WIDE, D), BF16),
        pltpu.VMEM((16, D), BF16),
        pltpu.VMEM((48, D), BF16),
    ]
    aliases = {}
    if first:
        results = [shape(D, WIDE), shape(RUNNING, D)]
    else:
        results = [shape(HALF, D), shape(HALF, D, BF16)]
        scratch += [pltpu.VMEM((D, WIDE), F32), pltpu.VMEM((RUNNING, D), F32)]
        scratch += [pltpu.VMEM((PACKED, D), F32)]
        in_specs += [whole(before[1]), whole(before[2]), pl.BlockSpec(memory_space=pl.ANY)]
        args += [before[1], before[2], before[0]]
        aliases = {len(args) - 1: 0}
    return pl.pallas_call(
        functools.partial(tower, scale, first),
        grid=(steps,),
        in_specs=in_specs,
        out_specs=[blocks] + [whole(r) for r in results],
        out_shape=[shape(rows, D)] + results,
        scratch_shapes=scratch,
        input_output_aliases=aliases,
        compiler_params=pltpu.CompilerParams(vmem_limit_bytes=60 << 20),
        cost_estimate=pl.CostEstimate(
            flops=steps * ROWS * 2500000,
            bytes_accessed=steps * ROWS * 2048,
            transcendentals=steps * ROWS * 1280,
        ),
        name="tower",
    )(*args)


def sum_over_chips(mine):
    count = lax.axis_size("batch")
    near = 8 if count == 16 else count
    groups = [[at * near + i for i in range(near)] for at in range(count // near)]
    swap = functools.partial(
        lax.all_to_all,
        axis_name="batch",
        split_axis=0,
        concat_axis=0,
        tiled=True,
        axis_index_groups=groups,
    )
    rows = mine.shape[0]
    share = swap(mine.reshape(near, -1, D))
    share = jnp.sum(share.astype(F32), axis=0).astype(BF16)
    if count == 2 * near:
        far = lax.ppermute(share, "batch", [(i, (i + near) % count) for i in range(count)])
        share = (share.astype(F32) + far.astype(F32)).astype(BF16)
    return swap(jnp.broadcast_to(share[None], (near, *share.shape))).reshape(rows, D)


def finish(core, stay, send):
    swap = [(0, 1), (1, 0)]
    mine = (stay + lax.ppermute(send, "grp", swap).astype(F32)).astype(BF16)
    mine = sum_over_chips(mine)
    other = pltpu.with_memory_space_constraint(lax.ppermute(mine, "grp", swap), pltpu.VMEM)
    sizes = (D, ACTIONS, 1, 1, D, D, 1, CODES, BINS)
    return pl.pallas_call(
        unpack,
        in_specs=[pl.BlockSpec(memory_space=pltpu.SMEM)] + [pl.BlockSpec(memory_space=pltpu.VMEM)] * 2,
        out_shape=[jax.ShapeDtypeStruct((n, D), F32) for n in sizes],
        scratch_shapes=[pltpu.VMEM((PACKED, D), F32)],
        name="unpack",
    )(core, mine, other)


def body(
    latent,
    future_latent,
    actions,
    codes,
    lengths,
    w_lat,
    w_act,
    gain_input,
    gain_block,
    w_one,
    w_two,
    gain_head,
    w_chance,
    w_value,
    w_target,
):
    rows = latent.shape[0]
    swap = [(0, 1), (1, 0)]
    moved_a = lax.ppermute(future_latent[:ROWS], "grp", swap)
    traj_total = lengths.shape[0] * lax.axis_size("grp") * lax.axis_size("batch")
    steps_idx = jnp.arange(UNROLL, dtype=jnp.int32)
    mask = (steps_idx[None, :] < lengths[:, None]).astype(jnp.int32).reshape(1, -1)
    index = (actions[None], codes[None], mask)
    moved_a, index, future_latent = lax.optimization_barrier((moved_a, index, future_latent))
    moved_b = lax.ppermute(future_latent, "grp", swap)
    weights = (
        w_lat,
        w_act,
        gain_input[None],
        gain_block[None],
        gain_head[None],
        w_one,
        w_two,
        w_chance.T,
        w_value.T,
        w_target.T,
    )
    scale = 1.0 / math.sqrt(traj_total)
    core = lax.axis_index("grp").astype(jnp.int32).reshape(1)
    part = run_tower(scale, core, 0, 1, latent, moved_a, index, weights, None)
    grad_latent, stay, send = run_tower(
        scale, core, 1, rows // ROWS - 1, latent, moved_b, index, weights, part
    )
    lat, act, gain_in, gain_bl, one, two, gain_he, chance, value = finish(core, stay, send)
    return (
        grad_latent,
        lat,
        act,
        gain_in[0],
        gain_bl[0],
        one,
        two,
        gain_he[0],
        chance.T,
        value.T,
    )


def solution(mesh):
    split = P(("grp", "batch"))
    rows = P(("grp", "batch"), None)
    in_specs = (rows, rows, split, split, split) + (P(),) * 10
    out_specs = (rows,) + (P(),) * 9
    return jax.shard_map(body, mesh=mesh, in_specs=in_specs, out_specs=out_specs, check_vma=False)
```

```python
import functools
import math

import jax
import jax.numpy as jnp
from jax import lax
from jax.experimental import pallas as pl
from jax.experimental.pallas import tpu as pltpu
from jax.sharding import PartitionSpec as P

D = 256
ACTIONS = 4
CODES = 32
BINS = 601
UNROLL = 5
EPSILON = 1e-05
WIDE = 640
CODE_AT = WIDE - CODES
ROWS = 1280
SUB = 640
ORDER = (
    "Atl", "Apre", "Aln1", "Aln2", "Ahid", "Atsm", "Abranch", "Alnh", "Bpre", "Bln1", "Alg",
    "Btl", "Alsm", "Bln2", "Agh", "Ahs", "Bhid", "Albh", "Btsm", "Bbranch", "Azed", "Atwo",
    "Blnh", "Ainn", "Aone", "Albb", "Blg", "Albf", "Alat", "Alats", "Blsm", "Bgh", "Bhs",
    "Blbh", "Bzed", "Btwo", "Binn", "Bone", "Blbb", "Blbf", "Blat", "Blats",
)
F32 = jnp.float32
BF16 = jnp.bfloat16

AT_TWO = 640
AT_ONE = 896
AT_LAT = 1152
AT_ACT = 1408
AT_GAIN = 1424
PACKED = 1536
HALF = PACKED // 2
RUN_TWO = 0
RUN_ONE = 256
RUN_LAT = 512
RUN_ACT = 768
RUN_GAIN = 784
RUNNING = 808


def dot(left, right, over_left, over_right):
    return lax.dot_general(
        left,
        right,
        (((over_left,), (over_right,)), ((), ())),
        preferred_element_type=F32,
    )


def normalize(value):
    center = value - jnp.mean(value, axis=1, keepdims=True)
    scaled = lax.rsqrt(jnp.mean(center * center, axis=1, keepdims=True) + EPSILON)
    return center * scaled, scaled


def norm_backward(grad, gain, normed, scaled):
    gained = grad * gain
    along = gained * normed
    centered = (
        gained
        - jnp.mean(gained, axis=1, keepdims=True)
        - normed * jnp.mean(along, axis=1, keepdims=True)
    )
    return scaled * centered, jnp.sum(along.reshape(-1, 8, D), axis=0)


def add_up(parts):
    return jnp.sum(parts.reshape(-1, 8, D), axis=0)


def pieces(value):
    return [value[:, at : at + 128] for at in range(0, WIDE, 128)]


def exps_and_sum(logits):
    top = jnp.max(functools.reduce(jnp.maximum, logits), axis=1, keepdims=True)
    exps = [jnp.exp(piece - top) for piece in logits]
    return exps, jnp.sum(functools.reduce(jnp.add, exps), axis=1, keepdims=True)


def tower(scale, first, first_block, *refs):
    (core, latent_ref, moved_ref, action_ref, code_ref, length_ref) = refs[:6]
    (w_lat, w_act, gain_in, gain_bl, gain_he, w_one, w_two, w_chance, w_value, w_target) = refs[6:16]
    if first:
        grad_latent, head_sums, sums, heads, encoder, acts, picks, spread = refs[16:]
    else:
        head_before, before, _, grad_latent, stay, send = refs[16:22]
        heads, encoder, acts, picks, spread, head_sums, sums, packed = refs[22:]
    rows = latent_ref.shape[0]

    @pl.when(pl.program_id(0) == 0)
    def _():
        gap = jnp.zeros((CODE_AT - BINS, D), F32)
        heads[...] = jnp.concatenate(
            [w_value[...].astype(F32), gap, w_chance[...].astype(F32)], axis=0
        ).astype(BF16)
        encoder[...] = jnp.concatenate(
            [w_target[...].astype(F32), jnp.zeros((WIDE - BINS, D), F32)], axis=0
        ).astype(BF16)
        acts[...] = jnp.concatenate(
            [w_act[...].astype(F32), jnp.zeros((16 - ACTIONS, D), F32)], axis=0
        ).astype(BF16)
        row = lax.broadcasted_iota(jnp.int32, (48, D), 0)
        col = lax.broadcasted_iota(jnp.int32, (48, D), 1)
        coded = (row < CODES) & (col == row + 128 - CODES)
        picks[...] = jnp.where(coded | ((row == CODES) & (col >= 128)), 1.0, 0.0).astype(BF16)
        row = UNROLL * lax.broadcasted_iota(jnp.int32, (128, SUB), 0)
        col = lax.broadcasted_iota(jnp.int32, (128, SUB), 1)
        spread[...] = jnp.where((col >= row) & (col < row + UNROLL), 1.0, 0.0).astype(BF16)
        head_sums[...] = jnp.zeros_like(head_sums) if first else head_before[...]
        sums[...] = jnp.zeros_like(sums) if first else before[...]

    lane = lax.broadcasted_iota(jnp.int32, (1, 128), 1)
    hide_value = jnp.where(lane < BINS - (WIDE - 128), 0.0, -1e30)
    hide_code = jnp.where(lane >= 128 - CODES, 0.0, -1e30)

    def target_step(logits):
        logits = pieces(logits)
        exps, total = exps_and_sum(logits[:4] + [logits[4] + hide_value])
        share = 1.0 / total
        return (jnp.concatenate([(e * share).astype(BF16) for e in exps], axis=1),)

    def one_part(at):
        span = slice(at, at + SUB)
        block = pl.program_id(0) + first_block
        lines = block * (rows // 128) + at // 128
        actions = jnp.concatenate(
            [action_ref[pl.ds(lines + i, 1), :] for i in range(SUB // 128)], axis=1
        )
        codes = jnp.concatenate(
            [code_ref[pl.ds(lines + i, 1), :] for i in range(SUB // 128)], axis=1
        )
        lengths = length_ref[pl.ds(block * (rows // SUB) + at // SUB, 1), :].astype(F32)
        lengths = dot(jnp.broadcast_to(lengths, (16, 128)).astype(BF16), spread[...], 1, 0)[0:1]
        unrolled = lax.rem(lax.broadcasted_iota(jnp.int32, (1, SUB), 1), UNROLL).astype(F32)
        mask = (unrolled < lengths).astype(F32)
        act_hot = lax.broadcasted_iota(jnp.int32, (16, SUB), 0) == actions
        act_hot = act_hot.astype(F32).astype(BF16)
        kind = lax.broadcasted_iota(jnp.int32, (48, SUB), 0)
        row_facts = jnp.where(kind == CODES, mask, (kind == codes).astype(F32)).astype(BF16)

        latent = latent_ref[span, :]
        def first_norm_step(pre):
            normed, scaled = normalize(pre)
            return normed, scaled, jnp.maximum(normed * gain_in[...], 0.0)

        def second_norm_step(state):
            normed, scaled = normalize(state)
            return normed, scaled, jnp.maximum(normed * gain_bl[...], 0.0).astype(BF16)

        def head_norm_step(state, branch):
            normed, scaled = normalize(state + branch)
            return normed, scaled, (normed * gain_he[...]).astype(BF16)

        def loss_step(logits, target, facts):
            code_hot = facts[:, :128]
            weight = facts[:, 128:] * scale
            target = [t.astype(F32) for t in pieces(target)]
            logits = pieces(logits)
            exps, total = exps_and_sum(logits[:4] + [logits[4] + hide_value])
            share = 1.0 / total
            code_exps, code_total = exps_and_sum([logits[4] + hide_code])
            grads = [e * share - t for e, t in zip(exps, target)]
            grads[4] = grads[4] + (code_exps[0] * (1.0 / code_total) - code_hot)
            return (jnp.concatenate([(g * weight).astype(BF16) for g in grads], axis=1),)

        def head_back_step(grad, normed, scaled):
            grad, along = norm_backward(grad, gain_he[...], normed, scaled)
            return grad, grad.astype(BF16), along

        def zed_back_step(grad, hidden):
            return (jnp.where(hidden > 0, grad.astype(BF16), jnp.zeros((), BF16)),)

        def block_back_step(grad, normed, scaled, state, grad_out):
            grad = jnp.where(normed > 0, grad, 0.0)
            through, along = norm_backward(grad, gain_bl[...], normed, scaled)
            return jnp.where(state > 0, grad_out + through, 0.0), along

        def first_back_step(grad, normed, scaled):
            grad, along = norm_backward(grad, gain_in[...], normed, scaled)
            return grad.astype(BF16), along

        pre = dot(latent, w_lat[...], 1, 0) + dot(act_hot, acts[...], 0, 0)
        yield "pre"
        first_norm, first_scale, state = first_norm_step(pre)
        yield "ln1"
        second_norm, second_scale, inner = second_norm_step(state)
        yield "ln2"
        hidden = jnp.maximum(dot(inner, w_one[...], 1, 0), 0.0).astype(BF16)
        yield "hid"
        branch = dot(hidden, w_two[...], 1, 0)
        yield "branch"
        head_norm, head_scale, head = head_norm_step(state, branch)
        yield "lnh"
        facts = dot(row_facts, picks[...], 0, 0)
        logits = dot(head, heads[...], 1, 1)
        yield "lg"
        (grad_logits,) = loss_step(logits, targets[at], facts)
        yield "lsm"
        grad_head = dot(grad_logits, heads[...], 1, 0)
        yield "gh"
        head_sums[...] += dot(head, grad_logits, 0, 0)
        yield "hs"
        grad_out, grad_branch, along = head_back_step(grad_head, head_norm, head_scale)
        sums[RUN_GAIN + 16 : RUN_GAIN + 24, :] += add_up(along)
        yield "lbh"
        (grad_zed,) = zed_back_step(dot(grad_branch, w_two[...], 1, 1), hidden)
        yield "zed"
        sums[RUN_TWO : RUN_TWO + 256, :] += dot(hidden, grad_branch, 0, 0)
        yield "two"
        grad_inner = dot(grad_zed, w_one[...], 1, 1)
        yield "inn"
        sums[RUN_ONE : RUN_ONE + 256, :] += dot(inner, grad_zed, 0, 0)
        yield "one"
        grad_first, along = block_back_step(grad_inner, second_norm, second_scale, state, grad_out)
        sums[RUN_GAIN + 8 : RUN_GAIN + 16, :] += add_up(along)
        yield "lbb"
        grad_pre, along = first_back_step(grad_first, first_norm, first_scale)
        sums[RUN_GAIN : RUN_GAIN + 8, :] += add_up(along)
        yield "lbf"
        grad_latent[span, :] = dot(grad_pre, w_lat[...], 1, 1)
        yield "lat"
        sums[RUN_LAT : RUN_LAT + 256, :] += dot(latent, grad_pre, 0, 0)
        sums[RUN_ACT : RUN_ACT + 16, :] += dot(act_hot, grad_pre, 1, 0)
        yield "lats"

    def one_target(at):
        logits = dot(moved_ref[at : at + SUB, :], encoder[...], 1, 1)
        yield "tl"
        (targets[at],) = target_step(logits)
        yield "tsm"

    targets = {}
    parts = {name: one_part(at) for name, at in zip("AB", range(0, rows, SUB))}
    goals = {name: one_target(at) for name, at in zip("AB", range(0, rows, SUB))}
    for word in ORDER:
        stages = goals if word[1:] in ("tl", "tsm") else parts
        assert next(stages[word[0]]) == word[1:]

    if not first:

        @pl.when(pl.program_id(0) == pl.num_programs(0) - 1)
        def _():
            packed[0:WIDE, :] = head_sums[...].T
            packed[AT_TWO:AT_GAIN, :] = sums[0:RUN_GAIN, :]
            gains = [
                jnp.sum(sums[RUN_GAIN + at : RUN_GAIN + at + 8, :], axis=0, keepdims=True) / gain[...]
                for at, gain in ((0, gain_in), (8, gain_bl), (16, gain_he))
            ]
            gains.append(jnp.zeros((PACKED - AT_GAIN - 3, D), F32))
            packed[AT_GAIN:, :] = jnp.concatenate(gains, axis=0)
            mine = pl.multiple_of(core[0] * HALF, HALF)
            stay[...] = packed[pl.ds(mine, HALF), :]
            send[...] = packed[pl.ds(HALF - mine, HALF), :].astype(BF16)


def unpack(core, mine, other, lat, act, gain_in, gain_bl, one, two, gain_he, chance, value, packed):
    at = pl.multiple_of(core[0] * HALF, HALF)
    packed[pl.ds(at, HALF), :] = mine[...].astype(F32)
    packed[pl.ds(HALF - at, HALF), :] = other[...].astype(F32)
    value[...] = packed[0:BINS, :]
    chance[...] = packed[CODE_AT:WIDE, :]
    two[...] = packed[AT_TWO : AT_TWO + D, :]
    one[...] = packed[AT_ONE : AT_ONE + D, :]
    lat[...] = packed[AT_LAT : AT_LAT + D, :]
    act[...] = packed[AT_ACT : AT_ACT + ACTIONS, :]
    gain_in[...] = packed[AT_GAIN : AT_GAIN + 1, :]
    gain_bl[...] = packed[AT_GAIN + 1 : AT_GAIN + 2, :]
    gain_he[...] = packed[AT_GAIN + 2 : AT_GAIN + 3, :]


def run_tower(scale, core, at, steps, latent, moved, index, weights, before):
    rows = latent.shape[0]

    def whole(array):
        zeros = (0,) * array.ndim
        return pl.BlockSpec(array.shape, lambda i: zeros)

    def shape(rows, cols, kind=F32):
        return jax.ShapeDtypeStruct((rows, cols), kind)

    blocks = pl.BlockSpec((ROWS, D), lambda i: (i + at, 0))
    first = before is None
    if first:
        moved = pltpu.with_memory_space_constraint(moved, pltpu.VMEM)
        moved_spec = pl.BlockSpec(memory_space=pltpu.VMEM)
    else:
        moved_spec = blocks
    in_specs = [pl.BlockSpec(memory_space=pltpu.SMEM), blocks, moved_spec]
    in_specs += [whole(part) for part in index]
    in_specs += [whole(w) for w in weights]
    args = [core, latent, moved, *index, *weights]
    scratch = [
        pltpu.VMEM((WIDE, D), BF16),
        pltpu.VMEM((WIDE, D), BF16),
        pltpu.VMEM((16, D), BF16),
        pltpu.VMEM((48, D), BF16),
        pltpu.VMEM((128, SUB), BF16),
    ]
    aliases = {}
    if first:
        results = [pltpu.VMEM((D, WIDE), F32), pltpu.VMEM((RUNNING, D), F32)]
    else:
        results = [pltpu.VMEM((HALF, D), F32), pltpu.VMEM((HALF, D), BF16)]
        scratch += [pltpu.VMEM((D, WIDE), F32), pltpu.VMEM((RUNNING, D), F32)]
        scratch += [pltpu.VMEM((PACKED, D), F32)]
        in_specs += [pl.BlockSpec(memory_space=pltpu.VMEM)] * 2 + [pl.BlockSpec(memory_space=pl.ANY)]
        args += [pltpu.with_memory_space_constraint(b, pltpu.VMEM) for b in before[1:]]
        args += [before[0]]
        aliases = {len(args) - 1: 0}
    return pl.pallas_call(
        functools.partial(tower, scale, first, at),
        grid=(steps,),
        in_specs=in_specs,
        out_specs=[blocks] + [pl.BlockSpec(memory_space=pltpu.VMEM)] * 2,
        out_shape=[shape(rows, D)] + results,
        scratch_shapes=scratch,
        input_output_aliases=aliases,
        compiler_params=pltpu.CompilerParams(vmem_limit_bytes=60 << 20),
        cost_estimate=pl.CostEstimate(
            flops=steps * ROWS * 2500000,
            bytes_accessed=steps * ROWS * 2048,
            transcendentals=steps * ROWS * 1280,
        ),
        name="tower",
    )(*args)


def sum_over_chips(mine):
    count = lax.axis_size("batch")
    near = 8 if count == 16 else count
    groups = [[at * near + i for i in range(near)] for at in range(count // near)]
    swap = functools.partial(
        lax.all_to_all,
        axis_name="batch",
        split_axis=0,
        concat_axis=0,
        tiled=True,
        axis_index_groups=groups,
    )
    rows = mine.shape[0]
    share = swap(mine.reshape(near, -1, D))
    share = jnp.sum(share.astype(F32), axis=0).astype(BF16)
    if count == 2 * near:
        far = lax.ppermute(share, "batch", [(i, (i + near) % count) for i in range(count)])
        share = (share.astype(F32) + far.astype(F32)).astype(BF16)
    return swap(jnp.broadcast_to(share[None], (near, *share.shape))).reshape(rows, D)


def finish(core, stay, send):
    swap = [(0, 1), (1, 0)]
    mine = (stay + lax.ppermute(send, "grp", swap).astype(F32)).astype(BF16)
    mine = sum_over_chips(mine)
    other = pltpu.with_memory_space_constraint(lax.ppermute(mine, "grp", swap), pltpu.VMEM)
    sizes = (D, ACTIONS, 1, 1, D, D, 1, CODES, BINS)
    return pl.pallas_call(
        unpack,
        in_specs=[pl.BlockSpec(memory_space=pltpu.SMEM)] + [pl.BlockSpec(memory_space=pltpu.VMEM)] * 2,
        out_shape=[jax.ShapeDtypeStruct((n, D), F32) for n in sizes],
        scratch_shapes=[pltpu.VMEM((PACKED, D), F32)],
        name="unpack",
    )(core, mine, other)


def body(
    latent,
    future_latent,
    actions,
    codes,
    lengths,
    w_lat,
    w_act,
    gain_input,
    gain_block,
    w_one,
    w_two,
    gain_head,
    w_chance,
    w_value,
    w_target,
):
    rows = latent.shape[0]
    swap = [(0, 1), (1, 0)]
    moved_a = lax.ppermute(future_latent[:ROWS], "grp", swap)
    traj_total = lengths.shape[0] * lax.axis_size("grp") * lax.axis_size("batch")
    index = (actions.reshape(-1, 128), codes.reshape(-1, 128), lengths.reshape(-1, SUB // UNROLL))
    moved_a, future_latent = lax.optimization_barrier((moved_a, future_latent))
    moved_b = lax.ppermute(future_latent, "grp", swap)
    weights = (
        w_lat,
        w_act,
        gain_input[None],
        gain_block[None],
        gain_head[None],
        w_one,
        w_two,
        w_chance.T,
        w_value.T,
        w_target.T,
    )
    scale = 1.0 / math.sqrt(traj_total)
    core = lax.axis_index("grp").astype(jnp.int32).reshape(1)
    part = run_tower(scale, core, 0, 1, latent, moved_a, index, weights, None)
    grad_latent, stay, send = run_tower(
        scale, core, 1, rows // ROWS - 1, latent, moved_b, index, weights, part
    )
    lat, act, gain_in, gain_bl, one, two, gain_he, chance, value = finish(core, stay, send)
    return (
        grad_latent,
        lat,
        act,
        gain_in[0],
        gain_bl[0],
        one,
        two,
        gain_he[0],
        chance.T,
        value.T,
    )


def solution(mesh):
    split = P(("grp", "batch"))
    rows = P(("grp", "batch"), None)
    in_specs = (rows, rows, split, split, split) + (P(),) * 10
    out_specs = (rows,) + (P(),) * 9
    return jax.shard_map(body, mesh=mesh, in_specs=in_specs, out_specs=out_specs, check_vma=False)
```

```python
import functools
import math

import jax
import jax.numpy as jnp
from jax import lax
from jax.experimental import pallas as pl
from jax.experimental.pallas import tpu as pltpu
from jax.sharding import PartitionSpec as P

D = 256
ACTIONS = 4
CODES = 32
BINS = 601
UNROLL = 5
EPSILON = 1e-05
WIDE = 640
CODE_AT = WIDE - CODES
ROWS = 1280
SUB = 640
ORDER = (
    "Atl", "Apre", "Aln1", "Aln2", "Ahid", "Atsm", "Abranch", "Alnh", "Bpre", "Bln1", "Alg",
    "Btl", "Alsm", "facts", "Bln2", "Agh", "Ahs", "Bhid", "Albh", "Btsm", "Bbranch", "Azed",
    "Atwo", "Blnh", "Ainn", "Aone", "Albb", "Blg", "Albf", "Alat", "Alats", "Blsm", "Bgh",
    "Bhs", "Blbh", "Bzed", "Btwo", "Binn", "Bone", "Blbb", "Blbf", "Blat", "Blats",
)
F32 = jnp.float32
BF16 = jnp.bfloat16

AT_TWO = 640
AT_ONE = 896
AT_LAT = 1152
AT_ACT = 1408
AT_GAIN = 1424
PACKED = 1536
HALF = PACKED // 2
RUN_TWO = 0
RUN_ONE = 256
RUN_LAT = 512
RUN_ACT = 768
RUN_GAIN = 784
RUNNING = 808


def dot(left, right, over_left, over_right):
    return lax.dot_general(
        left,
        right,
        (((over_left,), (over_right,)), ((), ())),
        preferred_element_type=F32,
    )


def normalize(value):
    center = value - jnp.mean(value, axis=1, keepdims=True)
    scaled = lax.rsqrt(jnp.mean(center * center, axis=1, keepdims=True) + EPSILON)
    return center * scaled, scaled


def norm_backward(grad, gain, normed, scaled):
    gained = grad * gain
    along = gained * normed
    centered = (
        gained
        - jnp.mean(gained, axis=1, keepdims=True)
        - normed * jnp.mean(along, axis=1, keepdims=True)
    )
    return scaled * centered, jnp.sum(along.reshape(-1, 8, D), axis=0)


def add_up(parts):
    return jnp.sum(parts.reshape(-1, 8, D), axis=0)


def pieces(value):
    return [value[:, at : at + 128] for at in range(0, WIDE, 128)]


def exps_and_sum(logits):
    top = jnp.max(functools.reduce(jnp.maximum, logits), axis=1, keepdims=True)
    exps = [jnp.exp(piece - top) for piece in logits]
    return exps, jnp.sum(functools.reduce(jnp.add, exps), axis=1, keepdims=True)


def tower(scale, first, first_block, last_block, *refs):
    (core, latent_ref, moved_ref, action_ref, code_ref, length_ref) = refs[:6]
    (w_lat, w_act, gain_in, gain_bl, gain_he, w_one, w_two, w_chance, w_value, w_target) = refs[6:16]
    if first:
        grad_latent, head_sums, sums, heads, encoder, acts, picks, spread = refs[16:24]
        act_hots, facts_kept = refs[24:]
    else:
        head_before, before, _, grad_latent, stay, send = refs[16:22]
        heads, encoder, acts, picks, spread, act_hots, facts_kept, head_sums, sums, packed = refs[22:]
    rows = latent_ref.shape[0]

    @pl.when(pl.program_id(0) == 0)
    def _():
        gap = jnp.zeros((CODE_AT - BINS, D), F32)
        heads[...] = jnp.concatenate(
            [w_value[...].astype(F32), gap, w_chance[...].astype(F32)], axis=0
        ).astype(BF16)
        encoder[...] = jnp.concatenate(
            [w_target[...].astype(F32), jnp.zeros((WIDE - BINS, D), F32)], axis=0
        ).astype(BF16)
        acts[...] = jnp.concatenate(
            [w_act[...].astype(F32), jnp.zeros((16 - ACTIONS, D), F32)], axis=0
        ).astype(BF16)
        row = lax.broadcasted_iota(jnp.int32, (48, D), 0)
        col = lax.broadcasted_iota(jnp.int32, (48, D), 1)
        coded = (row < CODES) & (col == row + 128 - CODES)
        picks[...] = jnp.where(coded | ((row == CODES) & (col >= 128)), 1.0, 0.0).astype(BF16)
        row = UNROLL * lax.broadcasted_iota(jnp.int32, (128, SUB), 0)
        col = lax.broadcasted_iota(jnp.int32, (128, SUB), 1)
        spread[...] = jnp.where((col >= row) & (col < row + UNROLL), 1.0, 0.0).astype(BF16)
        head_sums[...] = jnp.zeros_like(head_sums) if first else head_before[...]
        sums[...] = jnp.zeros_like(sums) if first else before[...]

    lane = lax.broadcasted_iota(jnp.int32, (1, 128), 1)
    hide_value = jnp.where(lane < BINS - (WIDE - 128), 0.0, -1e30)
    hide_code = jnp.where(lane >= 128 - CODES, 0.0, -1e30)

    def target_step(logits):
        logits = pieces(logits)
        exps, total = exps_and_sum(logits[:4] + [logits[4] + hide_value])
        share = 1.0 / total
        return (jnp.concatenate([(e * share).astype(BF16) for e in exps], axis=1),)

    now = lax.rem(pl.program_id(0), 2)

    def keep_facts(block, slot):
        for at in range(0, rows, SUB):
            span = slice(at, at + SUB)
            lines = block * (rows // 128) + at // 128
            actions = jnp.concatenate(
                [action_ref[pl.ds(lines + i, 1), :] for i in range(SUB // 128)], axis=1
            )
            codes = jnp.concatenate(
                [code_ref[pl.ds(lines + i, 1), :] for i in range(SUB // 128)], axis=1
            )
            lengths = length_ref[pl.ds(block * (rows // SUB) + at // SUB, 1), :].astype(F32)
            lengths = jnp.broadcast_to(lengths, (16, 128)).astype(BF16)
            lengths = dot(lengths, spread[...], 1, 0)[0:1]
            unrolled = lax.rem(lax.broadcasted_iota(jnp.int32, (1, SUB), 1), UNROLL).astype(F32)
            mask = (unrolled < lengths).astype(F32)
            hot = lax.broadcasted_iota(jnp.int32, (16, SUB), 0) == actions
            act_hots[slot, :, span] = hot.astype(F32).astype(BF16)
            kind = lax.broadcasted_iota(jnp.int32, (48, SUB), 0)
            facts_kept[slot, :, span] = jnp.where(
                kind == CODES, mask, (kind == codes).astype(F32)
            ).astype(BF16)

    this_block = pl.program_id(0) + first_block

    @pl.when(pl.program_id(0) == 0)
    def _():
        keep_facts(this_block, now)

    def one_part(at):
        span = slice(at, at + SUB)
        act_hot = act_hots[now, :, span]
        row_facts = facts_kept[now, :, span]
        latent = latent_ref[span, :]
        def first_norm_step(pre):
            normed, scaled = normalize(pre)
            return normed, scaled, jnp.maximum(normed * gain_in[...], 0.0)

        def second_norm_step(state):
            normed, scaled = normalize(state)
            return normed, scaled, jnp.maximum(normed * gain_bl[...], 0.0).astype(BF16)

        def head_norm_step(state, branch):
            normed, scaled = normalize(state + branch)
            return normed, scaled, (normed * gain_he[...]).astype(BF16)

        def loss_step(logits, target, facts):
            code_hot = facts[:, :128]
            weight = facts[:, 128:] * scale
            target = [t.astype(F32) for t in pieces(target)]
            logits = pieces(logits)
            exps, total = exps_and_sum(logits[:4] + [logits[4] + hide_value])
            share = 1.0 / total
            code_exps, code_total = exps_and_sum([logits[4] + hide_code])
            grads = [e * share - t for e, t in zip(exps, target)]
            grads[4] = grads[4] + (code_exps[0] * (1.0 / code_total) - code_hot)
            return (jnp.concatenate([(g * weight).astype(BF16) for g in grads], axis=1),)

        def head_back_step(grad, normed, scaled):
            grad, along = norm_backward(grad, gain_he[...], normed, scaled)
            return grad, grad.astype(BF16), along

        def zed_back_step(grad, hidden):
            return (jnp.where(hidden > 0, grad.astype(BF16), jnp.zeros((), BF16)),)

        def block_back_step(grad, normed, scaled, state, grad_out):
            grad = jnp.where(normed > 0, grad, 0.0)
            through, along = norm_backward(grad, gain_bl[...], normed, scaled)
            return jnp.where(state > 0, grad_out + through, 0.0), along

        def first_back_step(grad, normed, scaled):
            grad, along = norm_backward(grad, gain_in[...], normed, scaled)
            return grad.astype(BF16), along

        pre = dot(latent, w_lat[...], 1, 0) + dot(act_hot, acts[...], 0, 0)
        yield "pre"
        first_norm, first_scale, state = first_norm_step(pre)
        yield "ln1"
        second_norm, second_scale, inner = second_norm_step(state)
        yield "ln2"
        hidden = jnp.maximum(dot(inner, w_one[...], 1, 0), 0.0).astype(BF16)
        yield "hid"
        branch = dot(hidden, w_two[...], 1, 0)
        yield "branch"
        head_norm, head_scale, head = head_norm_step(state, branch)
        yield "lnh"
        facts = dot(row_facts, picks[...], 0, 0)
        logits = dot(head, heads[...], 1, 1)
        yield "lg"
        (grad_logits,) = loss_step(logits, targets[at], facts)
        yield "lsm"
        grad_head = dot(grad_logits, heads[...], 1, 0)
        yield "gh"
        head_sums[...] += dot(head, grad_logits, 0, 0)
        yield "hs"
        grad_out, grad_branch, along = head_back_step(grad_head, head_norm, head_scale)
        sums[RUN_GAIN + 16 : RUN_GAIN + 24, :] += add_up(along)
        yield "lbh"
        (grad_zed,) = zed_back_step(dot(grad_branch, w_two[...], 1, 1), hidden)
        yield "zed"
        sums[RUN_TWO : RUN_TWO + 256, :] += dot(hidden, grad_branch, 0, 0)
        yield "two"
        grad_inner = dot(grad_zed, w_one[...], 1, 1)
        yield "inn"
        sums[RUN_ONE : RUN_ONE + 256, :] += dot(inner, grad_zed, 0, 0)
        yield "one"
        grad_first, along = block_back_step(grad_inner, second_norm, second_scale, state, grad_out)
        sums[RUN_GAIN + 8 : RUN_GAIN + 16, :] += add_up(along)
        yield "lbb"
        grad_pre, along = first_back_step(grad_first, first_norm, first_scale)
        sums[RUN_GAIN : RUN_GAIN + 8, :] += add_up(along)
        yield "lbf"
        grad_latent[span, :] = dot(grad_pre, w_lat[...], 1, 1)
        yield "lat"
        sums[RUN_LAT : RUN_LAT + 256, :] += dot(latent, grad_pre, 0, 0)
        sums[RUN_ACT : RUN_ACT + 16, :] += dot(act_hot, grad_pre, 1, 0)
        yield "lats"

    def one_target(at):
        logits = dot(moved_ref[at : at + SUB, :], encoder[...], 1, 1)
        yield "tl"
        (targets[at],) = target_step(logits)
        yield "tsm"

    targets = {}
    parts = {name: one_part(at) for name, at in zip("AB", range(0, rows, SUB))}
    goals = {name: one_target(at) for name, at in zip("AB", range(0, rows, SUB))}
    for word in ORDER:
        if word == "facts":
            if not first:
                keep_facts(jnp.minimum(this_block + 1, last_block), 1 - now)
            continue
        stages = goals if word[1:] in ("tl", "tsm") else parts
        assert next(stages[word[0]]) == word[1:]

    if not first:

        @pl.when(pl.program_id(0) == pl.num_programs(0) - 1)
        def _():
            packed[0:WIDE, :] = head_sums[...].T
            packed[AT_TWO:AT_GAIN, :] = sums[0:RUN_GAIN, :]
            gains = [
                jnp.sum(sums[RUN_GAIN + at : RUN_GAIN + at + 8, :], axis=0, keepdims=True) / gain[...]
                for at, gain in ((0, gain_in), (8, gain_bl), (16, gain_he))
            ]
            gains.append(jnp.zeros((PACKED - AT_GAIN - 3, D), F32))
            packed[AT_GAIN:, :] = jnp.concatenate(gains, axis=0)
            mine = pl.multiple_of(core[0] * HALF, HALF)
            stay[...] = packed[pl.ds(mine, HALF), :]
            send[...] = packed[pl.ds(HALF - mine, HALF), :].astype(BF16)


def unpack(core, mine, other, lat, act, gain_in, gain_bl, one, two, gain_he, chance, value, packed):
    at = pl.multiple_of(core[0] * HALF, HALF)
    packed[pl.ds(at, HALF), :] = mine[...].astype(F32)
    packed[pl.ds(HALF - at, HALF), :] = other[...].astype(F32)
    value[...] = packed[0:BINS, :]
    chance[...] = packed[CODE_AT:WIDE, :]
    two[...] = packed[AT_TWO : AT_TWO + D, :]
    one[...] = packed[AT_ONE : AT_ONE + D, :]
    lat[...] = packed[AT_LAT : AT_LAT + D, :]
    act[...] = packed[AT_ACT : AT_ACT + ACTIONS, :]
    gain_in[...] = packed[AT_GAIN : AT_GAIN + 1, :]
    gain_bl[...] = packed[AT_GAIN + 1 : AT_GAIN + 2, :]
    gain_he[...] = packed[AT_GAIN + 2 : AT_GAIN + 3, :]


def run_tower(scale, core, at, steps, latent, moved, index, weights, before):
    rows = latent.shape[0]

    def whole(array):
        zeros = (0,) * array.ndim
        return pl.BlockSpec(array.shape, lambda i: zeros)

    def shape(rows, cols, kind=F32):
        return jax.ShapeDtypeStruct((rows, cols), kind)

    blocks = pl.BlockSpec((ROWS, D), lambda i: (i + at, 0))
    first = before is None
    if first:
        moved = pltpu.with_memory_space_constraint(moved, pltpu.VMEM)
        moved_spec = pl.BlockSpec(memory_space=pltpu.VMEM)
    else:
        moved_spec = blocks
    in_specs = [pl.BlockSpec(memory_space=pltpu.SMEM), blocks, moved_spec]
    in_specs += [whole(part) for part in index]
    in_specs += [whole(w) for w in weights]
    args = [core, latent, moved, *index, *weights]
    scratch = [
        pltpu.VMEM((WIDE, D), BF16),
        pltpu.VMEM((WIDE, D), BF16),
        pltpu.VMEM((16, D), BF16),
        pltpu.VMEM((48, D), BF16),
        pltpu.VMEM((128, SUB), BF16),
        pltpu.VMEM((2, 16, ROWS), BF16),
        pltpu.VMEM((2, 48, ROWS), BF16),
    ]
    aliases = {}
    if first:
        results = [pltpu.VMEM((D, WIDE), F32), pltpu.VMEM((RUNNING, D), F32)]
    else:
        results = [pltpu.VMEM((HALF, D), F32), pltpu.VMEM((HALF, D), BF16)]
        scratch += [pltpu.VMEM((D, WIDE), F32), pltpu.VMEM((RUNNING, D), F32)]
        scratch += [pltpu.VMEM((PACKED, D), F32)]
        in_specs += [pl.BlockSpec(memory_space=pltpu.VMEM)] * 2 + [pl.BlockSpec(memory_space=pl.ANY)]
        args += [pltpu.with_memory_space_constraint(b, pltpu.VMEM) for b in before[1:]]
        args += [before[0]]
        aliases = {len(args) - 1: 0}
    return pl.pallas_call(
        functools.partial(tower, scale, first, at, at + steps - 1),
        grid=(steps,),
        in_specs=in_specs,
        out_specs=[blocks] + [pl.BlockSpec(memory_space=pltpu.VMEM)] * 2,
        out_shape=[shape(rows, D)] + results,
        scratch_shapes=scratch,
        input_output_aliases=aliases,
        compiler_params=pltpu.CompilerParams(vmem_limit_bytes=60 << 20),
        cost_estimate=pl.CostEstimate(
            flops=steps * ROWS * 2500000,
            bytes_accessed=steps * ROWS * 2048,
            transcendentals=steps * ROWS * 1280,
        ),
        name="tower",
    )(*args)


def sum_over_chips(mine):
    count = lax.axis_size("batch")
    near = 8 if count == 16 else count
    groups = [[at * near + i for i in range(near)] for at in range(count // near)]
    swap = functools.partial(
        lax.all_to_all,
        axis_name="batch",
        split_axis=0,
        concat_axis=0,
        tiled=True,
        axis_index_groups=groups,
    )
    rows = mine.shape[0]
    share = swap(mine.reshape(near, -1, D))
    share = jnp.sum(share.astype(F32), axis=0).astype(BF16)
    if count == 2 * near:
        far = lax.ppermute(share, "batch", [(i, (i + near) % count) for i in range(count)])
        share = (share.astype(F32) + far.astype(F32)).astype(BF16)
    return swap(jnp.broadcast_to(share[None], (near, *share.shape))).reshape(rows, D)


def finish(core, stay, send):
    swap = [(0, 1), (1, 0)]
    mine = (stay + lax.ppermute(send, "grp", swap).astype(F32)).astype(BF16)
    mine = sum_over_chips(mine)
    other = pltpu.with_memory_space_constraint(lax.ppermute(mine, "grp", swap), pltpu.VMEM)
    sizes = (D, ACTIONS, 1, 1, D, D, 1, CODES, BINS)
    return pl.pallas_call(
        unpack,
        in_specs=[pl.BlockSpec(memory_space=pltpu.SMEM)] + [pl.BlockSpec(memory_space=pltpu.VMEM)] * 2,
        out_shape=[jax.ShapeDtypeStruct((n, D), F32) for n in sizes],
        scratch_shapes=[pltpu.VMEM((PACKED, D), F32)],
        name="unpack",
    )(core, mine, other)


def body(
    latent,
    future_latent,
    actions,
    codes,
    lengths,
    w_lat,
    w_act,
    gain_input,
    gain_block,
    w_one,
    w_two,
    gain_head,
    w_chance,
    w_value,
    w_target,
):
    rows = latent.shape[0]
    swap = [(0, 1), (1, 0)]
    moved_a = lax.ppermute(future_latent[:ROWS], "grp", swap)
    traj_total = lengths.shape[0] * lax.axis_size("grp") * lax.axis_size("batch")
    index = (actions.reshape(-1, 128), codes.reshape(-1, 128), lengths.reshape(-1, SUB // UNROLL))
    moved_a, future_latent = lax.optimization_barrier((moved_a, future_latent))
    moved_b = lax.ppermute(future_latent, "grp", swap)
    weights = (
        w_lat,
        w_act,
        gain_input[None],
        gain_block[None],
        gain_head[None],
        w_one,
        w_two,
        w_chance.T,
        w_value.T,
        w_target.T,
    )
    scale = 1.0 / math.sqrt(traj_total)
    core = lax.axis_index("grp").astype(jnp.int32).reshape(1)
    part = run_tower(scale, core, 0, 1, latent, moved_a, index, weights, None)
    grad_latent, stay, send = run_tower(
        scale, core, 1, rows // ROWS - 1, latent, moved_b, index, weights, part
    )
    lat, act, gain_in, gain_bl, one, two, gain_he, chance, value = finish(core, stay, send)
    return (
        grad_latent,
        lat,
        act,
        gain_in[0],
        gain_bl[0],
        one,
        two,
        gain_he[0],
        chance.T,
        value.T,
    )


def solution(mesh):
    split = P(("grp", "batch"))
    rows = P(("grp", "batch"), None)
    in_specs = (rows, rows, split, split, split) + (P(),) * 10
    out_specs = (rows,) + (P(),) * 9
    return jax.shard_map(body, mesh=mesh, in_specs=in_specs, out_specs=out_specs, check_vma=False)
```

```python
import functools
import math

import jax
import jax.numpy as jnp
from jax import lax
from jax.experimental import pallas as pl
from jax.experimental.pallas import tpu as pltpu
from jax.sharding import PartitionSpec as P

D = 256
ACTIONS = 4
CODES = 32
BINS = 601
UNROLL = 5
EPSILON = 1e-05
WIDE = 640
CODE_AT = WIDE - CODES
ROWS = 1280
SUB = 640
ORDER = (
    "Atl", "Apre", "Aln1", "Atsm", "Aln2", "Btl", "Ahid", "Abranch", "Bpre", "Alnh", "Bln1",
    "Alg", "Bln2", "Alsm", "facts", "Agh", "Ahs", "Btsm", "Albh", "Bhid", "Bbranch", "Azed",
    "Atwo", "Ainn", "Blnh", "Blg", "Aone", "Albb", "Albf", "Blsm", "Alat", "Alats", "Bgh",
    "Bhs", "Blbh", "Bzed", "Btwo", "Binn", "Bone", "Blbb", "Blbf", "Blat", "Blats",
)
F32 = jnp.float32
BF16 = jnp.bfloat16

AT_TWO = 640
AT_ONE = 896
AT_LAT = 1152
AT_ACT = 1408
AT_GAIN = 1424
PACKED = 1536
HALF = PACKED // 2
RUN_TWO = 0
RUN_ONE = 256
RUN_LAT = 512
RUN_ACT = 768
RUN_GAIN = 784
RUNNING = 808


def dot(left, right, over_left, over_right):
    return lax.dot_general(
        left,
        right,
        (((over_left,), (over_right,)), ((), ())),
        preferred_element_type=F32,
    )


def normalize(value):
    center = value - jnp.mean(value, axis=1, keepdims=True)
    scaled = lax.rsqrt(jnp.mean(center * center, axis=1, keepdims=True) + EPSILON)
    return center * scaled, scaled


def norm_backward(grad, gain, normed, scaled):
    gained = grad * gain
    along = gained * normed
    centered = (
        gained
        - jnp.mean(gained, axis=1, keepdims=True)
        - normed * jnp.mean(along, axis=1, keepdims=True)
    )
    return scaled * centered, jnp.sum(along.reshape(-1, 8, D), axis=0)


def add_up(parts):
    return jnp.sum(parts.reshape(-1, 8, D), axis=0)


def pieces(value):
    return [value[:, at : at + 128] for at in range(0, WIDE, 128)]


def exps_and_sum(logits):
    top = jnp.max(functools.reduce(jnp.maximum, logits), axis=1, keepdims=True)
    exps = [jnp.exp(piece - top) for piece in logits]
    return exps, jnp.sum(functools.reduce(jnp.add, exps), axis=1, keepdims=True)


def tower(scale, first, first_block, last_block, *refs):
    (core, latent_ref, moved_ref, action_ref, code_ref, length_ref) = refs[:6]
    (w_lat, gain_in, gain_bl, gain_he, w_one, w_two, heads, encoder, acts, picks, spread) = refs[6:17]
    if first:
        grad_latent, head_sums, sums, act_hots, facts_kept = refs[17:]
    else:
        head_before, before, _, grad_latent, stay, send = refs[17:23]
        act_hots, facts_kept, head_sums, sums, packed = refs[23:]
    rows = latent_ref.shape[0]

    @pl.when(pl.program_id(0) == 0)
    def _():
        head_sums[...] = jnp.zeros_like(head_sums) if first else head_before[...]
        sums[...] = jnp.zeros_like(sums) if first else before[...]

    lane = lax.broadcasted_iota(jnp.int32, (1, 128), 1)
    hide_value = jnp.where(lane < BINS - (WIDE - 128), 0.0, -1e30)
    hide_code = jnp.where(lane >= 128 - CODES, 0.0, -1e30)

    def target_step(logits):
        logits = pieces(logits)
        exps, total = exps_and_sum(logits[:4] + [logits[4] + hide_value])
        share = 1.0 / total
        return (jnp.concatenate([(e * share).astype(BF16) for e in exps], axis=1),)

    now = lax.rem(pl.program_id(0), 2)

    def keep_facts(block, slot):
        for at in range(0, rows, SUB):
            span = slice(at, at + SUB)
            lines = block * (rows // 128) + at // 128
            actions = jnp.concatenate(
                [action_ref[pl.ds(lines + i, 1), :] for i in range(SUB // 128)], axis=1
            )
            codes = jnp.concatenate(
                [code_ref[pl.ds(lines + i, 1), :] for i in range(SUB // 128)], axis=1
            )
            lengths = length_ref[pl.ds(block * (rows // SUB) + at // SUB, 1), :].astype(F32)
            lengths = jnp.broadcast_to(lengths, (16, 128)).astype(BF16)
            lengths = dot(lengths, spread[...], 1, 0)[0:1]
            unrolled = lax.rem(lax.broadcasted_iota(jnp.int32, (1, SUB), 1), UNROLL).astype(F32)
            mask = (unrolled < lengths).astype(F32)
            hot = lax.broadcasted_iota(jnp.int32, (16, SUB), 0) == actions
            act_hots[slot, :, span] = hot.astype(F32).astype(BF16)
            kind = lax.broadcasted_iota(jnp.int32, (48, SUB), 0)
            facts_kept[slot, :, span] = jnp.where(
                kind == CODES, mask, (kind == codes).astype(F32)
            ).astype(BF16)

    this_block = pl.program_id(0) + first_block

    @pl.when(pl.program_id(0) == 0)
    def _():
        keep_facts(this_block, now)

    def one_part(at):
        span = slice(at, at + SUB)
        act_hot = act_hots[now, :, span]
        row_facts = facts_kept[now, :, span]
        latent = latent_ref[span, :]
        def first_norm_step(pre):
            normed, scaled = normalize(pre)
            return normed, scaled, jnp.maximum(normed * gain_in[...], 0.0)

        def second_norm_step(state):
            normed, scaled = normalize(state)
            return normed, scaled, jnp.maximum(normed * gain_bl[...], 0.0).astype(BF16)

        def head_norm_step(state, branch):
            normed, scaled = normalize(state + branch)
            return normed, scaled, (normed * gain_he[...]).astype(BF16)

        def loss_step(logits, target, facts):
            code_hot = facts[:, :128]
            weight = facts[:, 128:] * scale
            target = [t.astype(F32) for t in pieces(target)]
            logits = pieces(logits)
            exps, total = exps_and_sum(logits[:4] + [logits[4] + hide_value])
            share = 1.0 / total
            code_exps, code_total = exps_and_sum([logits[4] + hide_code])
            grads = [e * share - t for e, t in zip(exps, target)]
            grads[4] = grads[4] + (code_exps[0] * (1.0 / code_total) - code_hot)
            return (jnp.concatenate([(g * weight).astype(BF16) for g in grads], axis=1),)

        def head_back_step(grad, normed, scaled):
            grad, along = norm_backward(grad, gain_he[...], normed, scaled)
            return grad, grad.astype(BF16), along

        def zed_back_step(grad, hidden):
            return (jnp.where(hidden > 0, grad.astype(BF16), jnp.zeros((), BF16)),)

        def block_back_step(grad, normed, scaled, state, grad_out):
            grad = jnp.where(normed > 0, grad, 0.0)
            through, along = norm_backward(grad, gain_bl[...], normed, scaled)
            return jnp.where(state > 0, grad_out + through, 0.0), along

        def first_back_step(grad, normed, scaled):
            grad, along = norm_backward(grad, gain_in[...], normed, scaled)
            return grad.astype(BF16), along

        pre = dot(latent, w_lat[...], 1, 0) + dot(act_hot, acts[...], 0, 0)
        yield "pre"
        first_norm, first_scale, state = first_norm_step(pre)
        yield "ln1"
        second_norm, second_scale, inner = second_norm_step(state)
        yield "ln2"
        hidden = jnp.maximum(dot(inner, w_one[...], 1, 0), 0.0).astype(BF16)
        yield "hid"
        branch = dot(hidden, w_two[...], 1, 0)
        yield "branch"
        head_norm, head_scale, head = head_norm_step(state, branch)
        yield "lnh"
        facts = dot(row_facts, picks[...], 0, 0)
        logits = dot(head, heads[...], 1, 1)
        yield "lg"
        (grad_logits,) = loss_step(logits, targets[at], facts)
        yield "lsm"
        grad_head = dot(grad_logits, heads[...], 1, 0)
        yield "gh"
        head_sums[...] += dot(head, grad_logits, 0, 0)
        yield "hs"
        grad_out, grad_branch, along = head_back_step(grad_head, head_norm, head_scale)
        sums[RUN_GAIN + 16 : RUN_GAIN + 24, :] += add_up(along)
        yield "lbh"
        (grad_zed,) = zed_back_step(dot(grad_branch, w_two[...], 1, 1), hidden)
        yield "zed"
        sums[RUN_TWO : RUN_TWO + 256, :] += dot(hidden, grad_branch, 0, 0)
        yield "two"
        grad_inner = dot(grad_zed, w_one[...], 1, 1)
        yield "inn"
        sums[RUN_ONE : RUN_ONE + 256, :] += dot(inner, grad_zed, 0, 0)
        yield "one"
        grad_first, along = block_back_step(grad_inner, second_norm, second_scale, state, grad_out)
        sums[RUN_GAIN + 8 : RUN_GAIN + 16, :] += add_up(along)
        yield "lbb"
        grad_pre, along = first_back_step(grad_first, first_norm, first_scale)
        sums[RUN_GAIN : RUN_GAIN + 8, :] += add_up(along)
        yield "lbf"
        grad_latent[span, :] = dot(grad_pre, w_lat[...], 1, 1)
        yield "lat"
        sums[RUN_LAT : RUN_LAT + 256, :] += dot(latent, grad_pre, 0, 0)
        sums[RUN_ACT : RUN_ACT + 16, :] += dot(act_hot, grad_pre, 1, 0)
        yield "lats"

    def one_target(at):
        logits = dot(moved_ref[at : at + SUB, :], encoder[...], 1, 1)
        yield "tl"
        (targets[at],) = target_step(logits)
        yield "tsm"

    targets = {}
    parts = {name: one_part(at) for name, at in zip("AB", range(0, rows, SUB))}
    goals = {name: one_target(at) for name, at in zip("AB", range(0, rows, SUB))}
    for word in ORDER:
        if word == "facts":
            if not first:
                keep_facts(jnp.minimum(this_block + 1, last_block), 1 - now)
            continue
        stages = goals if word[1:] in ("tl", "tsm") else parts
        assert next(stages[word[0]]) == word[1:]

    if not first:

        @pl.when(pl.program_id(0) == pl.num_programs(0) - 1)
        def _():
            packed[0:WIDE, :] = head_sums[...].T
            packed[AT_TWO:AT_GAIN, :] = sums[0:RUN_GAIN, :]
            gains = [
                jnp.sum(sums[RUN_GAIN + at : RUN_GAIN + at + 8, :], axis=0, keepdims=True) / gain[...]
                for at, gain in ((0, gain_in), (8, gain_bl), (16, gain_he))
            ]
            gains.append(jnp.zeros((PACKED - AT_GAIN - 3, D), F32))
            packed[AT_GAIN:, :] = jnp.concatenate(gains, axis=0)
            mine = pl.multiple_of(core[0] * HALF, HALF)
            stay[...] = packed[pl.ds(mine, HALF), :]
            send[...] = packed[pl.ds(HALF - mine, HALF), :].astype(BF16)


def unpack(core, mine, other, lat, act, gain_in, gain_bl, one, two, gain_he, chance, value, packed):
    at = pl.multiple_of(core[0] * HALF, HALF)
    packed[pl.ds(at, HALF), :] = mine[...].astype(F32)
    packed[pl.ds(HALF - at, HALF), :] = other[...].astype(F32)
    value[...] = packed[0:BINS, :]
    chance[...] = packed[CODE_AT:WIDE, :]
    two[...] = packed[AT_TWO : AT_TWO + D, :]
    one[...] = packed[AT_ONE : AT_ONE + D, :]
    lat[...] = packed[AT_LAT : AT_LAT + D, :]
    act[...] = packed[AT_ACT : AT_ACT + ACTIONS, :]
    gain_in[...] = packed[AT_GAIN : AT_GAIN + 1, :]
    gain_bl[...] = packed[AT_GAIN + 1 : AT_GAIN + 2, :]
    gain_he[...] = packed[AT_GAIN + 2 : AT_GAIN + 3, :]


def prepare(w_act, w_chance, w_value, w_target, heads, encoder, acts, picks, spread):
    gap = jnp.zeros((CODE_AT - BINS, D), F32)
    heads[...] = jnp.concatenate(
        [w_value[...].astype(F32), gap, w_chance[...].astype(F32)], axis=0
    ).astype(BF16)
    encoder[...] = jnp.concatenate(
        [w_target[...].astype(F32), jnp.zeros((WIDE - BINS, D), F32)], axis=0
    ).astype(BF16)
    acts[...] = jnp.concatenate(
        [w_act[...].astype(F32), jnp.zeros((16 - ACTIONS, D), F32)], axis=0
    ).astype(BF16)
    row = lax.broadcasted_iota(jnp.int32, (48, D), 0)
    col = lax.broadcasted_iota(jnp.int32, (48, D), 1)
    coded = (row < CODES) & (col == row + 128 - CODES)
    picks[...] = jnp.where(coded | ((row == CODES) & (col >= 128)), 1.0, 0.0).astype(BF16)
    row = UNROLL * lax.broadcasted_iota(jnp.int32, (128, SUB), 0)
    col = lax.broadcasted_iota(jnp.int32, (128, SUB), 1)
    spread[...] = jnp.where((col >= row) & (col < row + UNROLL), 1.0, 0.0).astype(BF16)


def prepare_weights(*weights):
    shapes = ((WIDE, D), (WIDE, D), (16, D), (48, D), (128, SUB))
    return pl.pallas_call(
        prepare,
        out_shape=[jax.ShapeDtypeStruct(s, BF16) for s in shapes],
        name="prepare",
    )(*weights)


def run_tower(scale, core, at, steps, latent, moved, index, weights, before):
    rows = latent.shape[0]

    def whole(array):
        zeros = (0,) * array.ndim
        return pl.BlockSpec(array.shape, lambda i: zeros)

    def shape(rows, cols, kind=F32):
        return jax.ShapeDtypeStruct((rows, cols), kind)

    blocks = pl.BlockSpec((ROWS, D), lambda i: (i + at, 0))
    first = before is None
    if first:
        moved = pltpu.with_memory_space_constraint(moved, pltpu.VMEM)
        moved_spec = pl.BlockSpec(memory_space=pltpu.VMEM)
    else:
        moved_spec = blocks
    in_specs = [pl.BlockSpec(memory_space=pltpu.SMEM), blocks, moved_spec]
    in_specs += [whole(part) for part in index]
    in_specs += [whole(w) for w in weights]
    args = [core, latent, moved, *index, *weights]
    scratch = [
        pltpu.VMEM((2, 16, ROWS), BF16),
        pltpu.VMEM((2, 48, ROWS), BF16),
    ]
    aliases = {}
    if first:
        results = [pltpu.VMEM((D, WIDE), F32), pltpu.VMEM((RUNNING, D), F32)]
    else:
        results = [pltpu.VMEM((HALF, D), F32), pltpu.VMEM((HALF, D), BF16)]
        scratch += [pltpu.VMEM((D, WIDE), F32), pltpu.VMEM((RUNNING, D), F32)]
        scratch += [pltpu.VMEM((PACKED, D), F32)]
        in_specs += [pl.BlockSpec(memory_space=pltpu.VMEM)] * 2 + [pl.BlockSpec(memory_space=pl.ANY)]
        args += [pltpu.with_memory_space_constraint(b, pltpu.VMEM) for b in before[1:]]
        args += [before[0]]
        aliases = {len(args) - 1: 0}
    return pl.pallas_call(
        functools.partial(tower, scale, first, at, at + steps - 1),
        grid=(steps,),
        in_specs=in_specs,
        out_specs=[blocks] + [pl.BlockSpec(memory_space=pltpu.VMEM)] * 2,
        out_shape=[shape(rows, D)] + results,
        scratch_shapes=scratch,
        input_output_aliases=aliases,
        compiler_params=pltpu.CompilerParams(vmem_limit_bytes=60 << 20),
        cost_estimate=pl.CostEstimate(
            flops=steps * ROWS * 2500000,
            bytes_accessed=steps * ROWS * 2048,
            transcendentals=steps * ROWS * 1280,
        ),
        name="tower",
    )(*args)


def sum_over_chips(mine):
    count = lax.axis_size("batch")
    near = 8 if count == 16 else count
    groups = [[at * near + i for i in range(near)] for at in range(count // near)]
    swap = functools.partial(
        lax.all_to_all,
        axis_name="batch",
        split_axis=0,
        concat_axis=0,
        tiled=True,
        axis_index_groups=groups,
    )
    rows = mine.shape[0]
    share = swap(mine.reshape(near, -1, D))
    share = jnp.sum(share.astype(F32), axis=0).astype(BF16)
    if count == 2 * near:
        far = lax.ppermute(share, "batch", [(i, (i + near) % count) for i in range(count)])
        share = (share.astype(F32) + far.astype(F32)).astype(BF16)
    return swap(jnp.broadcast_to(share[None], (near, *share.shape))).reshape(rows, D)


def finish(core, stay, send):
    swap = [(0, 1), (1, 0)]
    mine = (stay + lax.ppermute(send, "grp", swap).astype(F32)).astype(BF16)
    mine = sum_over_chips(mine)
    other = pltpu.with_memory_space_constraint(lax.ppermute(mine, "grp", swap), pltpu.VMEM)
    mine = pltpu.with_memory_space_constraint(mine, pltpu.VMEM)
    sizes = (D, ACTIONS, 1, 1, D, D, 1, CODES, BINS)
    return pl.pallas_call(
        unpack,
        in_specs=[pl.BlockSpec(memory_space=pltpu.SMEM)] + [pl.BlockSpec(memory_space=pltpu.VMEM)] * 2,
        out_shape=[jax.ShapeDtypeStruct((n, D), F32) for n in sizes],
        scratch_shapes=[pltpu.VMEM((PACKED, D), F32)],
        name="unpack",
    )(core, mine, other)


def body(
    latent,
    future_latent,
    actions,
    codes,
    lengths,
    w_lat,
    w_act,
    gain_input,
    gain_block,
    w_one,
    w_two,
    gain_head,
    w_chance,
    w_value,
    w_target,
):
    rows = latent.shape[0]
    swap = [(0, 1), (1, 0)]
    moved_a = lax.ppermute(future_latent[:ROWS], "grp", swap)
    traj_total = lengths.shape[0] * lax.axis_size("grp") * lax.axis_size("batch")
    index = (actions.reshape(-1, 128), codes.reshape(-1, 128), lengths.reshape(-1, SUB // UNROLL))
    ready = prepare_weights(w_act, w_chance.T, w_value.T, w_target.T)
    moved_a, ready, future_latent = lax.optimization_barrier((moved_a, ready, future_latent))
    weights = (w_lat, gain_input[None], gain_block[None], gain_head[None], w_one, w_two, *ready)
    moved_b = lax.ppermute(future_latent, "grp", swap)
    scale = 1.0 / math.sqrt(traj_total)
    core = lax.axis_index("grp").astype(jnp.int32).reshape(1)
    part = run_tower(scale, core, 0, 1, latent, moved_a, index, weights, None)
    grad_latent, stay, send = run_tower(
        scale, core, 1, rows // ROWS - 1, latent, moved_b, index, weights, part
    )
    lat, act, gain_in, gain_bl, one, two, gain_he, chance, value = finish(core, stay, send)
    return (
        grad_latent,
        lat,
        act,
        gain_in[0],
        gain_bl[0],
        one,
        two,
        gain_he[0],
        chance.T,
        value.T,
    )


def solution(mesh):
    split = P(("grp", "batch"))
    rows = P(("grp", "batch"), None)
    in_specs = (rows, rows, split, split, split) + (P(),) * 10
    out_specs = (rows,) + (P(),) * 9
    return jax.shard_map(body, mesh=mesh, in_specs=in_specs, out_specs=out_specs, check_vma=False)
```

```python
import functools
import math

import jax
import jax.numpy as jnp
from jax import lax
from jax.experimental import pallas as pl
from jax.experimental.pallas import tpu as pltpu
from jax.sharding import PartitionSpec as P

D = 256
ACTIONS = 4
CODES = 32
BINS = 601
UNROLL = 5
EPSILON = 1e-05
WIDE = 640
CODE_AT = WIDE - CODES
ROWS = 1280
SUB = 640
ORDER = (
    "Apre", "Atl", "Bpre", "Aln1", "Aln2", "Atsm", "Ahid", "Abranch", "Btl", "Alnh", "Alg",
    "Bln1", "Bln2", "Alsm", "facts", "Agh", "Ahs", "Bhid", "Albh", "Bbranch", "Azed", "Atwo",
    "Blnh", "Ainn", "Aone", "Blg", "Btsm", "Blsm", "Albb", "Albf", "Alat", "Alats", "Bgh",
    "Bhs", "Blbh", "Bzed", "Btwo", "Binn", "Bone", "Blbb", "Blbf", "Blat", "Blats",
)
F32 = jnp.float32
BF16 = jnp.bfloat16

AT_TWO = 640
AT_ONE = 896
AT_LAT = 1152
AT_ACT = 1408
AT_GAIN = 1424
PACKED = 1536
HALF = PACKED // 2
RUN_TWO = 0
RUN_ONE = 256
RUN_LAT = 512
RUN_ACT = 768
RUN_GAIN = 784
RUNNING = 808


def dot(left, right, over_left, over_right):
    return lax.dot_general(
        left,
        right,
        (((over_left,), (over_right,)), ((), ())),
        preferred_element_type=F32,
    )


def normalize(value):
    center = value - jnp.mean(value, axis=1, keepdims=True)
    scaled = lax.rsqrt(jnp.mean(center * center, axis=1, keepdims=True) + EPSILON)
    return center * scaled, scaled


def norm_backward(grad, gain, normed, scaled):
    gained = grad * gain
    along = gained * normed
    centered = (
        gained
        - jnp.mean(gained, axis=1, keepdims=True)
        - normed * jnp.mean(along, axis=1, keepdims=True)
    )
    return scaled * centered, jnp.sum(along.reshape(-1, 8, D), axis=0)


def add_up(parts):
    return jnp.sum(parts.reshape(-1, 8, D), axis=0)


def pieces(value):
    return [value[:, at : at + 128] for at in range(0, WIDE, 128)]


def exps_and_sum(logits):
    top = jnp.max(functools.reduce(jnp.maximum, logits), axis=1, keepdims=True)
    exps = [jnp.exp(piece - top) for piece in logits]
    return exps, jnp.sum(functools.reduce(jnp.add, exps), axis=1, keepdims=True)


def tower(scale, first, first_block, last_block, *refs):
    (core, latent_ref, moved_ref, action_ref, code_ref, length_ref) = refs[:6]
    (w_lat, gain_in, gain_bl, gain_he, w_one, w_two, heads, encoder, acts, picks, spread) = refs[6:17]
    if first:
        grad_latent, head_sums, sums, act_hots, facts_kept = refs[17:]
    else:
        head_before, before, _, grad_latent, stay, send = refs[17:23]
        act_hots, facts_kept, head_sums, sums, packed = refs[23:]
    rows = latent_ref.shape[0]

    @pl.when(pl.program_id(0) == 0)
    def _():
        head_sums[...] = jnp.zeros_like(head_sums) if first else head_before[...]
        sums[...] = jnp.zeros_like(sums) if first else before[...]

    lane = lax.broadcasted_iota(jnp.int32, (1, 128), 1)
    hide_value = jnp.where(lane < BINS - (WIDE - 128), 0.0, -1e30)
    hide_code = jnp.where(lane >= 128 - CODES, 0.0, -1e30)

    def target_step(logits):
        logits = pieces(logits)
        exps, total = exps_and_sum(logits[:4] + [logits[4] + hide_value])
        share = 1.0 / total
        return (jnp.concatenate([(e * share).astype(BF16) for e in exps], axis=1),)

    now = lax.rem(pl.program_id(0), 2)

    def keep_facts(block, slot):
        for at in range(0, rows, SUB):
            span = slice(at, at + SUB)
            lines = block * (rows // 128) + at // 128
            actions = jnp.concatenate(
                [action_ref[pl.ds(lines + i, 1), :] for i in range(SUB // 128)], axis=1
            )
            codes = jnp.concatenate(
                [code_ref[pl.ds(lines + i, 1), :] for i in range(SUB // 128)], axis=1
            )
            lengths = length_ref[pl.ds(block * (rows // SUB) + at // SUB, 1), :].astype(F32)
            lengths = jnp.broadcast_to(lengths, (16, 128)).astype(BF16)
            lengths = dot(lengths, spread[...], 1, 0)[0:1]
            unrolled = lax.rem(lax.broadcasted_iota(jnp.int32, (1, SUB), 1), UNROLL).astype(F32)
            mask = (unrolled < lengths).astype(F32)
            hot = lax.broadcasted_iota(jnp.int32, (16, SUB), 0) == actions
            act_hots[slot, :, span] = hot.astype(F32).astype(BF16)
            kind = lax.broadcasted_iota(jnp.int32, (48, SUB), 0)
            facts_kept[slot, :, span] = jnp.where(
                kind == CODES, mask, (kind == codes).astype(F32)
            ).astype(BF16)

    this_block = pl.program_id(0) + first_block

    @pl.when(pl.program_id(0) == 0)
    def _():
        keep_facts(this_block, now)

    def one_part(at):
        span = slice(at, at + SUB)
        act_hot = act_hots[now, :, span]
        row_facts = facts_kept[now, :, span]
        latent = latent_ref[span, :]
        def first_norm_step(pre):
            normed, scaled = normalize(pre)
            return normed, scaled, jnp.maximum(normed * gain_in[...], 0.0)

        def second_norm_step(state):
            normed, scaled = normalize(state)
            return normed, scaled, jnp.maximum(normed * gain_bl[...], 0.0).astype(BF16)

        def head_norm_step(state, branch):
            normed, scaled = normalize(state + branch)
            return normed, scaled, (normed * gain_he[...]).astype(BF16)

        def loss_step(logits, target, facts):
            code_hot = facts[:, :128]
            weight = facts[:, 128:] * scale
            target = [t.astype(F32) for t in pieces(target)]
            logits = pieces(logits)
            exps, total = exps_and_sum(logits[:4] + [logits[4] + hide_value])
            share = 1.0 / total
            code_exps, code_total = exps_and_sum([logits[4] + hide_code])
            grads = [e * share - t for e, t in zip(exps, target)]
            grads[4] = grads[4] + (code_exps[0] * (1.0 / code_total) - code_hot)
            return (jnp.concatenate([(g * weight).astype(BF16) for g in grads], axis=1),)

        def head_back_step(grad, normed, scaled):
            grad, along = norm_backward(grad, gain_he[...], normed, scaled)
            return grad, grad.astype(BF16), along

        def zed_back_step(grad, hidden):
            return (jnp.where(hidden > 0, grad.astype(BF16), jnp.zeros((), BF16)),)

        def block_back_step(grad, normed, scaled, state, grad_out):
            grad = jnp.where(normed > 0, grad, 0.0)
            through, along = norm_backward(grad, gain_bl[...], normed, scaled)
            return jnp.where(state > 0, grad_out + through, 0.0), along

        def first_back_step(grad, normed, scaled):
            grad, along = norm_backward(grad, gain_in[...], normed, scaled)
            return grad.astype(BF16), along

        pre = dot(latent, w_lat[...], 1, 0) + dot(act_hot, acts[...], 0, 0)
        yield "pre"
        first_norm, first_scale, state = first_norm_step(pre)
        yield "ln1"
        second_norm, second_scale, inner = second_norm_step(state)
        yield "ln2"
        hidden = jnp.maximum(dot(inner, w_one[...], 1, 0), 0.0).astype(BF16)
        yield "hid"
        branch = dot(hidden, w_two[...], 1, 0)
        yield "branch"
        head_norm, head_scale, head = head_norm_step(state, branch)
        yield "lnh"
        facts = dot(row_facts, picks[...], 0, 0)
        logits = dot(head, heads[...], 1, 1)
        yield "lg"
        (grad_logits,) = loss_step(logits, targets[at], facts)
        yield "lsm"
        grad_head = dot(grad_logits, heads[...], 1, 0)
        yield "gh"
        head_sums[...] += dot(head, grad_logits, 0, 0)
        yield "hs"
        grad_out, grad_branch, along = head_back_step(grad_head, head_norm, head_scale)
        sums[RUN_GAIN + 16 : RUN_GAIN + 24, :] += add_up(along)
        yield "lbh"
        (grad_zed,) = zed_back_step(dot(grad_branch, w_two[...], 1, 1), hidden)
        yield "zed"
        sums[RUN_TWO : RUN_TWO + 256, :] += dot(hidden, grad_branch, 0, 0)
        yield "two"
        grad_inner = dot(grad_zed, w_one[...], 1, 1)
        yield "inn"
        sums[RUN_ONE : RUN_ONE + 256, :] += dot(inner, grad_zed, 0, 0)
        yield "one"
        grad_first, along = block_back_step(grad_inner, second_norm, second_scale, state, grad_out)
        sums[RUN_GAIN + 8 : RUN_GAIN + 16, :] += add_up(along)
        yield "lbb"
        grad_pre, along = first_back_step(grad_first, first_norm, first_scale)
        sums[RUN_GAIN : RUN_GAIN + 8, :] += add_up(along)
        yield "lbf"
        grad_latent[span, :] = dot(grad_pre, w_lat[...], 1, 1)
        yield "lat"
        sums[RUN_LAT : RUN_LAT + 256, :] += dot(latent, grad_pre, 0, 0)
        sums[RUN_ACT : RUN_ACT + 16, :] += dot(act_hot, grad_pre, 1, 0)
        yield "lats"

    def one_target(at):
        logits = dot(moved_ref[at : at + SUB, :], encoder[...], 1, 1)
        yield "tl"
        (targets[at],) = target_step(logits)
        yield "tsm"

    targets = {}
    parts = {name: one_part(at) for name, at in zip("AB", range(0, rows, SUB))}
    goals = {name: one_target(at) for name, at in zip("AB", range(0, rows, SUB))}
    for word in ORDER:
        if word == "facts":
            if not first:
                keep_facts(jnp.minimum(this_block + 1, last_block), 1 - now)
            continue
        stages = goals if word[1:] in ("tl", "tsm") else parts
        assert next(stages[word[0]]) == word[1:]

    if not first:

        @pl.when(pl.program_id(0) == pl.num_programs(0) - 1)
        def _():
            packed[0:WIDE, :] = head_sums[...].T
            packed[AT_TWO:AT_GAIN, :] = sums[0:RUN_GAIN, :]
            gains = [
                jnp.sum(sums[RUN_GAIN + at : RUN_GAIN + at + 8, :], axis=0, keepdims=True) / gain[...]
                for at, gain in ((0, gain_in), (8, gain_bl), (16, gain_he))
            ]
            gains.append(jnp.zeros((PACKED - AT_GAIN - 3, D), F32))
            packed[AT_GAIN:, :] = jnp.concatenate(gains, axis=0)
            mine = pl.multiple_of(core[0] * HALF, HALF)
            stay[...] = packed[pl.ds(mine, HALF), :]
            send[...] = packed[pl.ds(HALF - mine, HALF), :].astype(BF16)


def unpack(core, mine, other, lat, act, gain_in, gain_bl, one, two, gain_he, chance, value, packed):
    at = pl.multiple_of(core[0] * HALF, HALF)
    packed[pl.ds(at, HALF), :] = mine[...].astype(F32)
    packed[pl.ds(HALF - at, HALF), :] = other[...].astype(F32)
    value[...] = packed[0:BINS, :]
    chance[...] = packed[CODE_AT:WIDE, :]
    two[...] = packed[AT_TWO : AT_TWO + D, :]
    one[...] = packed[AT_ONE : AT_ONE + D, :]
    lat[...] = packed[AT_LAT : AT_LAT + D, :]
    act[...] = packed[AT_ACT : AT_ACT + ACTIONS, :]
    gain_in[...] = packed[AT_GAIN : AT_GAIN + 1, :]
    gain_bl[...] = packed[AT_GAIN + 1 : AT_GAIN + 2, :]
    gain_he[...] = packed[AT_GAIN + 2 : AT_GAIN + 3, :]


def prepare(w_act, w_chance, w_value, w_target, heads, encoder, acts, picks, spread):
    gap = jnp.zeros((CODE_AT - BINS, D), F32)
    heads[...] = jnp.concatenate(
        [w_value[...].astype(F32), gap, w_chance[...].astype(F32)], axis=0
    ).astype(BF16)
    encoder[...] = jnp.concatenate(
        [w_target[...].astype(F32), jnp.zeros((WIDE - BINS, D), F32)], axis=0
    ).astype(BF16)
    acts[...] = jnp.concatenate(
        [w_act[...].astype(F32), jnp.zeros((16 - ACTIONS, D), F32)], axis=0
    ).astype(BF16)
    row = lax.broadcasted_iota(jnp.int32, (48, D), 0)
    col = lax.broadcasted_iota(jnp.int32, (48, D), 1)
    coded = (row < CODES) & (col == row + 128 - CODES)
    picks[...] = jnp.where(coded | ((row == CODES) & (col >= 128)), 1.0, 0.0).astype(BF16)
    row = UNROLL * lax.broadcasted_iota(jnp.int32, (128, SUB), 0)
    col = lax.broadcasted_iota(jnp.int32, (128, SUB), 1)
    spread[...] = jnp.where((col >= row) & (col < row + UNROLL), 1.0, 0.0).astype(BF16)


def prepare_weights(*weights):
    shapes = ((WIDE, D), (WIDE, D), (16, D), (48, D), (128, SUB))
    return pl.pallas_call(
        prepare,
        out_shape=[jax.ShapeDtypeStruct(s, BF16) for s in shapes],
        name="prepare",
    )(*weights)


def run_tower(scale, core, at, steps, latent, moved, index, weights, before):
    rows = latent.shape[0]

    def whole(array):
        zeros = (0,) * array.ndim
        return pl.BlockSpec(array.shape, lambda i: zeros)

    def shape(rows, cols, kind=F32):
        return jax.ShapeDtypeStruct((rows, cols), kind)

    blocks = pl.BlockSpec((ROWS, D), lambda i: (i + at, 0))
    first = before is None
    if first:
        moved = pltpu.with_memory_space_constraint(moved, pltpu.VMEM)
        moved_spec = pl.BlockSpec(memory_space=pltpu.VMEM)
    else:
        moved_spec = blocks
    in_specs = [pl.BlockSpec(memory_space=pltpu.SMEM), blocks, moved_spec]
    in_specs += [whole(part) for part in index]
    in_specs += [whole(w) for w in weights]
    args = [core, latent, moved, *index, *weights]
    scratch = [
        pltpu.VMEM((2, 16, ROWS), BF16),
        pltpu.VMEM((2, 48, ROWS), BF16),
    ]
    aliases = {}
    if first:
        results = [pltpu.VMEM((D, WIDE), F32), pltpu.VMEM((RUNNING, D), F32)]
    else:
        results = [pltpu.VMEM((HALF, D), F32), pltpu.VMEM((HALF, D), BF16)]
        scratch += [pltpu.VMEM((D, WIDE), F32), pltpu.VMEM((RUNNING, D), F32)]
        scratch += [pltpu.VMEM((PACKED, D), F32)]
        in_specs += [pl.BlockSpec(memory_space=pltpu.VMEM)] * 2 + [pl.BlockSpec(memory_space=pl.ANY)]
        args += [pltpu.with_memory_space_constraint(b, pltpu.VMEM) for b in before[1:]]
        args += [before[0]]
        aliases = {len(args) - 1: 0}
    return pl.pallas_call(
        functools.partial(tower, scale, first, at, at + steps - 1),
        grid=(steps,),
        in_specs=in_specs,
        out_specs=[blocks] + [pl.BlockSpec(memory_space=pltpu.VMEM)] * 2,
        out_shape=[shape(rows, D)] + results,
        scratch_shapes=scratch,
        input_output_aliases=aliases,
        compiler_params=pltpu.CompilerParams(vmem_limit_bytes=60 << 20),
        cost_estimate=pl.CostEstimate(
            flops=steps * ROWS * 2500000,
            bytes_accessed=steps * ROWS * 2048,
            transcendentals=steps * ROWS * 1280,
        ),
        name="tower",
    )(*args)


def sum_over_chips(mine):
    count = lax.axis_size("batch")
    near = 8 if count == 16 else count
    groups = [[at * near + i for i in range(near)] for at in range(count // near)]
    swap = functools.partial(
        lax.all_to_all,
        axis_name="batch",
        split_axis=0,
        concat_axis=0,
        tiled=True,
        axis_index_groups=groups,
    )
    rows = mine.shape[0]
    share = swap(mine.reshape(near, -1, D))
    share = jnp.sum(share.astype(F32), axis=0).astype(BF16)
    if count == 2 * near:
        far = lax.ppermute(share, "batch", [(i, (i + near) % count) for i in range(count)])
        share = (share.astype(F32) + far.astype(F32)).astype(BF16)
    return swap(jnp.broadcast_to(share[None], (near, *share.shape))).reshape(rows, D)


def finish(core, stay, send):
    swap = [(0, 1), (1, 0)]
    mine = (stay + lax.ppermute(send, "grp", swap).astype(F32)).astype(BF16)
    mine = sum_over_chips(mine)
    other = pltpu.with_memory_space_constraint(lax.ppermute(mine, "grp", swap), pltpu.VMEM)
    mine = pltpu.with_memory_space_constraint(mine, pltpu.VMEM)
    sizes = (D, ACTIONS, 1, 1, D, D, 1, CODES, BINS)
    return pl.pallas_call(
        unpack,
        in_specs=[pl.BlockSpec(memory_space=pltpu.SMEM)] + [pl.BlockSpec(memory_space=pltpu.VMEM)] * 2,
        out_shape=[jax.ShapeDtypeStruct((n, D), F32) for n in sizes],
        scratch_shapes=[pltpu.VMEM((PACKED, D), F32)],
        name="unpack",
    )(core, mine, other)


def body(
    latent,
    future_latent,
    actions,
    codes,
    lengths,
    w_lat,
    w_act,
    gain_input,
    gain_block,
    w_one,
    w_two,
    gain_head,
    w_chance,
    w_value,
    w_target,
):
    rows = latent.shape[0]
    swap = [(0, 1), (1, 0)]
    moved_a = lax.ppermute(future_latent[:ROWS], "grp", swap)
    traj_total = lengths.shape[0] * lax.axis_size("grp") * lax.axis_size("batch")
    index = (actions.reshape(-1, 128), codes.reshape(-1, 128), lengths.reshape(-1, SUB // UNROLL))
    ready = prepare_weights(w_act, w_chance.T, w_value.T, w_target.T)
    moved_a, ready, future_latent = lax.optimization_barrier((moved_a, ready, future_latent))
    weights = (w_lat, gain_input[None], gain_block[None], gain_head[None], w_one, w_two, *ready)
    moved_b = lax.ppermute(future_latent, "grp", swap)
    scale = 1.0 / math.sqrt(traj_total)
    core = lax.axis_index("grp").astype(jnp.int32).reshape(1)
    part = run_tower(scale, core, 0, 1, latent, moved_a, index, weights, None)
    grad_latent, stay, send = run_tower(
        scale, core, 1, rows // ROWS - 1, latent, moved_b, index, weights, part
    )
    lat, act, gain_in, gain_bl, one, two, gain_he, chance, value = finish(core, stay, send)
    return (
        grad_latent,
        lat,
        act,
        gain_in[0],
        gain_bl[0],
        one,
        two,
        gain_he[0],
        chance.T,
        value.T,
    )


def solution(mesh):
    split = P(("grp", "batch"))
    rows = P(("grp", "batch"), None)
    in_specs = (rows, rows, split, split, split) + (P(),) * 10
    out_specs = (rows,) + (P(),) * 9
    return jax.shard_map(body, mesh=mesh, in_specs=in_specs, out_specs=out_specs, check_vma=False)
```
